256 devices in a mesh: dp: 64 (over x, z, core), mp: 4 (over y).
Axes of the slice: x: 4, y: 4, z: 8, core: 2. Of those that a mesh axis runs over, the one named last changes fastest.
Arguments:
- history: bfloat16 [1024, 32, 1024], P('dp', None, 'mp'), may hold values from -6 to 6
- lengths: int32 [1024], replicated, may hold values from 1 to 32, 16384 in all
- source: int32 [1024], replicated, may hold values from 0 to 1023, as said below
- owners: int32 [32768, 8], P(('dp', 'mp')), may hold values from 0 to 255, all different within a row; in each aligned block of 128 rows (0 to 127, 128 to 255, ...) at most 6 rows name the same one
- item_rows: int32 [32768, 8], P(('dp', 'mp')), may hold values from 0 to 511
- catalogue: bfloat16 [131072, 1024], P(('dp', 'mp')), may hold values from -6 to 6
- w_in: bfloat16 [4, 1024, 1024], P(None, None, 'mp'), may hold values from -0.1875 to 0.1875
- w_out: bfloat16 [1024, 1024], P('mp'), may hold values from -0.1875 to 0.1875
Outputs:
- w_in_grad: float32 [4, 1024, 1024], P(None, 'dp', 'mp')
- w_out_grad: float32 [1024, 1024], P('mp', 'dp')
- cat_grad: float32 [131072, 1024], P(('dp', 'mp'))
The draws below stay inside these ranges and needn't reach their ends.
Inputs may be any that keep to these rules, and one draw needn't show every extreme that they name: `source`: a permutation; balanced slot k lies on index k // 16 of dp, and the 16 histories that start on one index of dp go to one index of dp at most (16 + 64 - 1) // 64 at a time, that many for some index. Each event names 8 different owners, column 0 the positive item's; the events of one device (aligned blocks of 128) name one owner at most 6 times.
All inputs are finite; a program needn't handle non-finite values.
Results may differ from the reference program's by a relative error of at most 0.017.
Values may be sent and summed in bfloat16 or wider, within the bound.
A program may use at most 128 MiB of HBM per device.

```python
import math
import jax
import jax.numpy as jnp
import numpy as np
from jax import lax

D = 1024
H = 8
HD = 1024
LMAX = 32
SEQ_DEV = 16
TOP = 8
CAT_DEV = 512
SEQS = 1024
EVENTS = 32768
EQ = 128
CAP = 6
CAT = 131072
DEVICES = 256


def draw_source(key, part):
    devices_n = SEQS // SEQ_DEV
    key_order, key_offset, key_slots = jax.random.split(jax.random.fold_in(key, 17), 3)
    order = jax.random.permutation(key_order, devices_n).astype(jnp.int32)
    offset = jax.random.permutation(key_offset, devices_n).astype(jnp.int32)
    slot_ids = jnp.arange(SEQ_DEV, dtype=jnp.int32)
    target = order[(offset[:, None] + slot_ids[None, :]) % devices_n].reshape(-1)
    noise = jax.random.permutation(key_slots, SEQS).astype(jnp.int32)
    scores = target * SEQS + noise
    rank_of = jnp.argsort(jnp.argsort(scores)).astype(jnp.int32)
    flat_src = jnp.arange(SEQS, dtype=jnp.int32)
    return jnp.zeros((SEQS,), jnp.int32).at[rank_of].set(flat_src)


def set_ends(entries, key, least, high):
    spot = [jax.random.randint(jax.random.fold_in(key, axis), (), 0, length) for axis, length in enumerate(entries.shape)]
    main_axis = entries.shape.index(max(entries.shape))
    neighbour = spot[:main_axis] + [(spot[main_axis] + 1) % entries.shape[main_axis]] + spot[main_axis + 1:]
    return entries.at[tuple(spot)].set(least).at[tuple(neighbour)].set(high)


def block_levels(own_key, dims, cuts, smallest, largest):
    loudness = 1.0
    for axis_at, blocks in cuts:
        heights = jax.random.uniform(jax.random.fold_in(jax.random.fold_in(own_key, 6), axis_at), (blocks,), jnp.float32, smallest / len(cuts), largest / len(cuts))
        loudness = loudness * jnp.repeat(jnp.exp(heights), dims[axis_at] // blocks).reshape((-1,) + (1,) * (len(dims) - 1 - axis_at))
    return loudness


def split_up(amount, total, bound, skew):
    loads = [(1 << 20) // math.isqrt(rank ** skew) + 1 for rank in range(2, amount + 1)]
    rest, given = total - bound - (amount - 1), [1] * (amount - 1)
    while rest > 0:
        movable = [i for i in range(amount - 1) if given[i] < bound]
        mass, budget = sum([loads[i] for i in movable]), rest
        for i in movable:
            more = min(bound - given[i], max(1, budget * loads[i] // mass), rest)
            given[i] = given[i] + more
            rest = rest - more
    return np.array([bound] + given)


def uneven(rng, count, total, limit, lean):
    if count == 2:
        one = jax.random.randint(rng, (), max(1, total - limit), min(limit, total - 1) + 1)
        return jnp.stack([one, total - one])
    sizes = jnp.asarray(split_up(count, total, limit, lean), jnp.int32)
    pairs = (count - 1) // 2
    giver, receiver = sizes[1:1 + 2 * pairs:2], sizes[2:2 + 2 * pairs:2]
    room = jnp.minimum(giver - 1, limit - receiver)
    shifted = jax.random.randint(jax.random.fold_in(rng, 1), (pairs,), 0, 1 << 20) % (room + 1)
    sizes = sizes.at[1:1 + 2 * pairs:2].set(giver - shifted).at[2:2 + 2 * pairs:2].set(receiver + shifted)
    return sizes[jax.random.permutation(jax.random.fold_in(rng, 2), count)]


def shared_out(own_key, own, number, rows, count, top, reach, lean):
    ranking = jax.random.permutation(own_key, count)
    crowded, usual = portions_of(count, rows * top, reach, lean, True), portions_of(count, rows * top, reach, lean, False)
    places = jnp.arange(count)

    def named(sizes, turn):
        used = int((sizes > 0).sum())
        fixed = max(1, used // 4)
        shifted = fixed + (places - fixed + turn * (used - fixed)) % max(1, count - fixed)
        return jnp.zeros((count,), jnp.int32).at[ranking[jnp.where(places < fixed, places, shifted)]].set(jnp.asarray(sizes, jnp.int32))

    sizes = jnp.where(number % 4 == 0, named(crowded, number // 4), named(usual, number - number // 4 - 1))
    mixed = jax.random.permutation(jax.random.fold_in(own, 3), count)
    giver, sink = mixed[0:count // 2 * 2:2], mixed[1:count // 2 * 2:2]
    slack = jnp.minimum(sizes[giver] - 1, reach - sizes[sink]) // 2
    slack = jnp.where((giver == ranking[0]) | (sink == ranking[0]) | (sizes[sink] == 0), 0, jnp.maximum(slack, 0))
    shifted = jax.random.randint(jax.random.fold_in(own, 4), (count // 2,), 0, 1 << 20) % (slack + 1)
    sizes = sizes.at[giver].add(-shifted).at[sink].add(shifted)
    members = jnp.searchsorted(jnp.cumsum(sizes), jnp.arange(rows * top), side="right").astype(jnp.int32)
    listing = members.reshape(top, rows).T
    listing = listing[jax.random.permutation(jax.random.fold_in(own, 1), rows)]
    turn = jax.random.randint(jax.random.fold_in(own, 2), (rows, 1), 0, top)
    return jnp.take_along_axis(listing, (jnp.arange(top)[None, :] + turn) % top, axis=1)


def portions_of(number_of, total, most, skew, full):
    weights = [(1 << 20) // math.isqrt(grade ** skew) + 1 for grade in range(1, number_of + 1)]
    largest = most if full else min(most, max(-(-total // number_of), total * weights[0] // sum(weights)))
    least = 1 if total - largest >= number_of - 1 else 0
    given, rest = [largest] + [least] * (number_of - 1), total - largest - least * (number_of - 1)
    while rest > 0:
        free = [i for i in range(1, number_of) if given[i] < largest] or [i for i in range(1, number_of) if given[i] < most]
        mass, left = sum([weights[i] for i in free]), rest
        for i in free:
            addition = min(most - given[i], max(1, left * weights[i] // mass), rest)
            given[i] = given[i] + addition
            rest = rest - addition
    return np.array(given)


def normal_values(own_key, dims, scale, reach, cuts=(), held_as=jnp.bfloat16):
    gain = block_levels(own_key, dims, cuts, -0.22, 0.18) if cuts else 1.0
    result = jax.random.normal(own_key, dims, jnp.float32) * scale * gain
    return jnp.minimum(jnp.maximum(result, -reach), reach).astype(held_as)


def setup_inputs(seed: int = 0) -> dict:
    key_list = jax.random.split(jax.random.key(seed), 9)
    history = normal_values(key_list[0], (SEQS, LMAX, D), 1.0, 6.0, ((0, 64), (2, 4)))
    lengths = uneven(key_list[1], SEQS, SEQS * LMAX // 2, LMAX, 2).astype(jnp.int32)
    source = draw_source(jax.random.fold_in(key_list[8], 71), 0)
    owners_keys = jax.random.split(jax.random.fold_in(key_list[3], 1), EVENTS // EQ)
    owners_turns = jax.random.permutation(jax.random.fold_in(key_list[3], 3), EVENTS // EQ)
    owners = jax.vmap(lambda own, number: shared_out(jax.random.fold_in(key_list[3], 2), own, number, EQ, DEVICES, TOP, CAP, 1))(owners_keys, owners_turns).reshape((EVENTS, TOP))
    item_rows = set_ends(jax.random.randint(key_list[4], (EVENTS, TOP), 0, CAT_DEV), jax.random.fold_in(key_list[4], 1), 0, CAT_DEV - 1).astype(jnp.int32)
    catalogue = normal_values(key_list[5], (CAT, D), 1.0, 6.0, ((0, 256),))
    w_in = normal_values(key_list[6], (4, D, HD), D ** -0.5, 0.1875, ((2, 4),))
    w_out = normal_values(key_list[7], (HD, D), HD ** -0.5, 0.1875, ((0, 4),))
    return {"history": history, "lengths": lengths, "source": source, "owners": owners, "item_rows": item_rows, "catalogue": catalogue, "w_in": w_in, "w_out": w_out}


cosine_divisor = 0.05
epsilon_norm = 1e-05
epsilon_unit = 1e-06

def normalize(rows_in):
    centered = rows_in - lax.optimization_barrier(jnp.mean(rows_in, axis=-1, keepdims=True))
    spread = lax.optimization_barrier(jnp.mean(centered * centered, axis=-1, keepdims=True))
    return centered / jnp.sqrt(spread + epsilon_norm)

def attend(projected, length_here):
    gating = projected[0].astype(jnp.float32)
    values = projected[1].astype(jnp.float32)
    queries = projected[2].astype(jnp.float32)
    key_rows = projected[3].astype(jnp.float32)
    steps_n = projected.shape[1]
    scores = jnp.einsum('thd,shd->hts', queries, key_rows) / jnp.sqrt(jnp.float32(projected.shape[3]))
    places = jnp.arange(steps_n, dtype=jnp.int32)
    allowed = (places[None, :] <= places[:, None]) & (places[None, :] < length_here)
    weights = jnp.where(allowed[None], jax.nn.silu(scores) / length_here.astype(jnp.float32), 0.0).astype(jnp.bfloat16)
    mixed_out = jnp.einsum('hts,shd->thd', weights.astype(jnp.float32), values)
    return (normalize(mixed_out) * gating).astype(jnp.bfloat16)

def loss_block(out_rows, valid_rows, fetched):
    out_norm = jnp.sqrt(lax.optimization_barrier(jnp.sum(out_rows * out_rows, axis=-1, keepdims=True)) + epsilon_unit)
    request_unit_vector = out_rows / out_norm
    item_f = fetched.astype(jnp.float32)
    item_norm = jnp.sqrt(lax.optimization_barrier(jnp.sum(item_f * item_f, axis=-1, keepdims=True)) + epsilon_unit)
    catalog_unit_vector = item_f / item_norm
    cosine_match_raw = jnp.einsum('qn,qgn->qg', request_unit_vector, catalog_unit_vector) / cosine_divisor
    expo = jnp.exp(cosine_match_raw)
    probs = expo / lax.optimization_barrier(jnp.sum(expo, axis=-1, keepdims=True))
    column = jnp.arange(cosine_match_raw.shape[1], dtype=jnp.int32)
    exponent_shares = (probs - (column[None, :] == 0).astype(jnp.float32)) * valid_rows[:, None].astype(jnp.float32)
    request_unit_vector_slope = jnp.einsum('as,asy->ay', exponent_shares, catalog_unit_vector) / cosine_divisor
    out_grad = (request_unit_vector_slope - request_unit_vector * lax.optimization_barrier(jnp.sum(request_unit_vector * request_unit_vector_slope, axis=-1, keepdims=True))) / out_norm
    catalog_unit_vector_slope = exponent_shares[:, :, None] * request_unit_vector[:, None, :] / cosine_divisor
    item_grad = (catalog_unit_vector_slope - catalog_unit_vector * lax.optimization_barrier(jnp.sum(catalog_unit_vector * catalog_unit_vector_slope, axis=-1, keepdims=True))) / item_norm
    return (out_grad, item_grad)

def silu_slope(preact):
    sigma = jax.nn.sigmoid(preact)
    return sigma * (1.0 + preact * (1.0 - sigma))

def reference(history, lengths, source, owners, item_rows, catalogue, w_in, w_out):
    seq_total, steps_n, width = history.shape
    balanced = history[source]
    counts = lengths[source]
    flat_rows = balanced.reshape(seq_total * steps_n, width)
    normed = normalize(flat_rows.astype(jnp.float32)).astype(jnp.bfloat16)
    preact = jnp.stack([jnp.dot(normed, w_in[part_id], preferred_element_type=jnp.float32) for part_id in range(4)])
    projected = jax.nn.silu(preact).astype(jnp.bfloat16)
    all_width = w_in.shape[2]
    head_size = all_width // H
    grouped = projected.reshape(4, seq_total, steps_n, H, head_size).transpose(1, 0, 2, 3, 4)

    def run_all(inputs):
        return lax.map(lambda pair: attend(pair[0], pair[1]), (inputs, counts))
    gated, back = jax.vjp(run_all, grouped)
    gated_flat = gated.reshape(seq_total * steps_n, all_width)
    output = flat_rows.astype(jnp.float32) + jnp.dot(gated_flat, w_out, preferred_element_type=jnp.float32)
    valid = (jnp.arange(steps_n, dtype=jnp.int32)[None, :] < counts[:, None]).reshape(-1)
    items = owners * CAT_DEV + item_rows
    blocks = seq_total * steps_n // EQ
    top_n = owners.shape[1]

    def one_block(carried, inputs):
        out_rows, valid_rows, item_ids = inputs
        fetched = catalogue[item_ids]
        out_grad, item_grad = loss_block(out_rows, valid_rows, fetched)
        carried = carried.at[item_ids.reshape(-1)].add(item_grad.reshape(-1, width))
        return (carried, out_grad)
    cat_grad, out_grads = lax.scan(one_block, jnp.zeros((catalogue.shape[0], width), jnp.float32), (output.reshape(blocks, EQ, width), valid.reshape(blocks, EQ), items.reshape(blocks, EQ, top_n)))
    out_cotangent = out_grads.reshape(seq_total * steps_n, width).astype(jnp.bfloat16)
    w_out_grad = jnp.dot(gated_flat.T, out_cotangent, preferred_element_type=jnp.float32)
    gated_cotangent = jnp.dot(out_cotangent, w_out.T, preferred_element_type=jnp.float32).astype(jnp.bfloat16)
    grouped_cotangent, = back(gated_cotangent.reshape(seq_total, steps_n, H, head_size))
    projected_cotangent = grouped_cotangent.transpose(1, 0, 2, 3, 4).reshape(4, seq_total * steps_n, all_width)
    preact_cotangent = (projected_cotangent.astype(jnp.float32) * silu_slope(preact)).astype(jnp.bfloat16)
    w_in_grad = jnp.stack([jnp.dot(normed.T, preact_cotangent[part_id], preferred_element_type=jnp.float32) for part_id in range(4)])
    return (w_in_grad, w_out_grad, cat_grad)
```

```python
import functools

import jax
import jax.numpy as jnp
from jax import lax
from jax.experimental import pallas as pl
from jax.experimental.pallas import tpu as pltpu
from jax.sharding import Mesh, PartitionSpec as P

DH = 128
CAP = 6
MESH = pl.DeviceIdType.MESH
F32 = jnp.float32
BF16 = jnp.bfloat16

cosine_divisor = 0.05
epsilon_norm = 1e-05
epsilon_unit = 1e-06

VM = pl.BlockSpec(memory_space=pltpu.VMEM)
SM = pl.BlockSpec(memory_space=pltpu.SMEM)


def sds(shape, dtype):
    return jax.ShapeDtypeStruct(shape, dtype)


def params(**kw):
    return pltpu.CompilerParams(vmem_limit_bytes=60 * 1024 * 1024, **kw)


def mp_id(m):
    return (lax.axis_index("x"), lax.axis_index("z"), lax.axis_index("c"), m)


def enter(peers):
    barrier = pltpu.get_barrier_semaphore()
    for peer in peers:
        pl.semaphore_signal(barrier, inc=1, device_id=peer, device_id_type=MESH)
    pl.semaphore_wait(barrier, len(peers))


def slots_kernel(own_ref, row_ref, want_ref, event_ref, rank_ref, col_ref):
    owners_n, events = rank_ref.shape
    who = lax.broadcasted_iota(jnp.int32, (owners_n, events), 0)
    named = jnp.zeros((owners_n, events), F32)
    rows = jnp.zeros((owners_n, events), jnp.int32)
    cols = jnp.zeros((owners_n, events), jnp.int32)
    for j in range(own_ref.shape[0]):
        mask = own_ref[j : j + 1, :] == who
        named = jnp.where(mask, 1.0, named)
        rows = jnp.where(mask, row_ref[j : j + 1, :], rows)
        cols = jnp.where(mask, j, cols)
    before = (
        lax.broadcasted_iota(jnp.int32, (events, events), 0)
        < lax.broadcasted_iota(jnp.int32, (events, events), 1)
    ).astype(F32)
    rank = jnp.dot(
        named.astype(BF16), before.astype(BF16), preferred_element_type=F32
    ).astype(jnp.int32)
    rank = jnp.where(named > 0.0, rank, -1)
    rank_ref[...] = rank
    col_ref[...] = cols
    event = lax.broadcasted_iota(jnp.int32, (owners_n, events), 1)
    lane = lax.broadcasted_iota(jnp.int32, want_ref.shape, 1)
    want = jnp.full(want_ref.shape, -1, jnp.int32)
    chosen = jnp.zeros(want_ref.shape, jnp.int32)
    for r in range(CAP):
        here = rank == r
        row_r = jnp.max(jnp.where(here, rows, -1), axis=1, keepdims=True)
        event_r = jnp.max(jnp.where(here, event, 0), axis=1, keepdims=True)
        want = jnp.where(lane == r, row_r, want)
        chosen = jnp.where(lane == r, event_r, chosen)
    want_ref[...] = want
    event_ref[...] = chosen


def slots(owners_t, rows_t, dev_count):
    events = owners_t.shape[1]
    table = sds((dev_count, 128), jnp.int32)
    wide = sds((dev_count, events), jnp.int32)
    return pl.pallas_call(
        slots_kernel,
        out_shape=(table, table, wide, wide),
        in_specs=[VM] * 2,
        out_specs=(VM,) * 4,
        compiler_params=params(),
        name="slots",
    )(owners_t, rows_t)


def gather_kernel(idx_ref, table_ref, out_ref):
    def one(s, carry):
        for r in range(CAP):
            out_ref[s, r] = table_ref[jnp.maximum(idx_ref[s, r], 0)]
        return carry

    lax.fori_loop(0, out_ref.shape[0], one, 0, unroll=4)


def gather_rows(idx, table):
    n = idx.shape[0]
    return pl.pallas_call(
        gather_kernel,
        out_shape=sds((n, CAP) + table.shape[1:], table.dtype),
        in_specs=[SM, VM],
        out_specs=VM,
        compiler_params=params(),
        name="gather_rows",
    )(idx, table)


def pick_kernel(idx_ref, table_ref, out_ref):
    def one(s, carry):
        out_ref[s] = table_ref[idx_ref[s]]
        return carry

    lax.fori_loop(0, out_ref.shape[0], one, 0, unroll=4)


def pick_blocks(idx, table):
    n = idx.shape[0]
    return pl.pallas_call(
        pick_kernel,
        out_shape=sds((n,) + table.shape[1:], table.dtype),
        in_specs=[SM, VM],
        out_specs=VM,
        compiler_params=params(),
        name="pick_blocks",
    )(idx, table)


def loss_kernel(
    items_ref, out_ref, rank_ref, col_ref, valid_ref, grad_ref, coef_ref, flat, mat, cosine, expo
):
    n, _, lanes_hi, lanes = items_ref.shape
    out = out_ref[...]
    inv_out = 1.0 / jnp.sqrt(jnp.sum(out * out, axis=-1, keepdims=True) + epsilon_unit)
    unit = out * inv_out
    unit_b = unit.astype(BF16)
    rank = rank_ref[...]
    total = jnp.zeros((1, rank.shape[1]), F32)
    inverse = []
    for r in range(CAP):
        flat[...] = items_ref[:, r].astype(F32).reshape(n * lanes_hi, lanes)
        squares = jnp.zeros((n, lanes), F32)
        for c in range(lanes_hi):
            chunk = flat[pl.ds(c, n, stride=lanes_hi), :]
            squares = squares + chunk * chunk
            mat[r, :, c * lanes : (c + 1) * lanes] = chunk.astype(BF16)
        inv = 1.0 / jnp.sqrt(jnp.sum(squares, axis=-1, keepdims=True) + epsilon_unit)
        inverse.append(inv)
        dots = lax.dot_general(
            mat[r], unit_b, (((1,), (1,)), ((), ())), preferred_element_type=F32
        )
        cos = dots * inv
        ex = jnp.where(rank == r, jnp.exp(cos / cosine_divisor), 0.0)
        cosine[r] = cos
        expo[r] = ex
        total = total + jnp.sum(ex, axis=0, keepdims=True)
    valid = valid_ref[0:1, :]
    scale = valid / total
    first = (col_ref[...] == 0).astype(F32) * valid
    lane = lax.broadcasted_iota(jnp.int32, coef_ref.shape, 1)
    coef = jnp.zeros(coef_ref.shape, F32)
    slope = jnp.zeros(out.shape, F32)
    for r in range(CAP):
        share = expo[r] * scale - jnp.where(rank == r, first, 0.0)
        weight = share * (inverse[r] / cosine_divisor)
        slope = slope + lax.dot_general(
            weight.astype(BF16), mat[r], (((0,), (0,)), ((), ())), preferred_element_type=F32
        )
        a = jnp.sum(weight, axis=-1, keepdims=True)
        b = jnp.sum(weight * cosine[r], axis=-1, keepdims=True) * inverse[r]
        coef = jnp.where(lane == r, a, coef)
        coef = jnp.where(lane == r + 8, b, coef)
    coef_ref[...] = coef
    along = jnp.sum(unit * slope, axis=-1, keepdims=True)
    grad_ref[...] = ((slope - unit * along) * inv_out).astype(BF16)


def loss_call(items, out_rows, rank, col, valid):
    n = items.shape[0]
    events, width = out_rows.shape
    return pl.pallas_call(
        loss_kernel,
        out_shape=(sds((events, width), BF16), sds((n, 128), F32)),
        in_specs=[VM] * 5,
        out_specs=(VM,) * 2,
        scratch_shapes=[
            pltpu.VMEM((n * items.shape[2], items.shape[3]), F32),
            pltpu.VMEM((CAP, n, width), BF16),
            pltpu.VMEM((CAP, n, events), F32),
            pltpu.VMEM((CAP, n, events), F32),
        ],
        compiler_params=params(),
        name="loss",
    )(items, out_rows, rank, col, valid)


def catalogue_kernel(units_ref, want_ref, coef_ref, cat_ref, out_ref, flat, mat, hot, side):
    n, _, lanes_hi, lanes = units_ref.shape
    rows = cat_ref.shape[0]
    want = want_ref[...]
    coef = coef_ref[...]
    row = lax.broadcasted_iota(jnp.int32, (n, rows), 1)
    lane = lax.broadcasted_iota(jnp.int32, (n, lanes), 1)
    for r in range(CAP):
        flat[...] = units_ref[:, r].astype(F32).reshape(n * lanes_hi, lanes)
        a = coef[:, r : r + 1]
        b = coef[:, r + 8 : r + 9]
        high = b.astype(BF16).astype(F32)
        span = pl.ds(r * n, n)
        for c in range(lanes_hi):
            chunk = flat[pl.ds(c, n, stride=lanes_hi), :]
            mat[span, c * lanes : (c + 1) * lanes] = (chunk * a).astype(BF16)
        side[span, :] = jnp.where(
            lane == 0, high, jnp.where(lane == 1, b - high, 0.0)
        ).astype(BF16)
        hot[span, :] = (want[:, r : r + 1] == row).astype(F32).astype(BF16)
    over = (((0,), (0,)), ((), ()))
    both = lax.dot_general(hot[...], side[...], over, preferred_element_type=F32)
    b_row = both[:, 0:1] + both[:, 1:2]
    for c in range(0, cat_ref.shape[1], 256):
        part = lax.dot_general(hot[...], mat[:, c : c + 256], over, preferred_element_type=F32)
        out_ref[:, c : c + 256] = part - b_row * cat_ref[:, c : c + 256].astype(F32)


def catalogue_call(units, want, coef, catalogue):
    n = units.shape[0]
    rows, width = catalogue.shape
    return pl.pallas_call(
        catalogue_kernel,
        out_shape=sds((rows, width), F32),
        in_specs=[VM] * 4,
        out_specs=VM,
        scratch_shapes=[
            pltpu.VMEM((n * units.shape[2], units.shape[3]), F32),
            pltpu.VMEM((CAP * n, width), BF16),
            pltpu.VMEM((CAP * n, rows), BF16),
            pltpu.VMEM((CAP * n, 128), BF16),
        ],
        compiler_params=params(),
        name="catalogue_grad",
    )(units, want, coef, catalogue)


def gather_mp_kernel(n, by_column, x_ref, out_ref, send, recv, local):
    me = lax.axis_index("mp")
    peers = [lax.rem(me + k, n) for k in range(1, n)]
    enter([mp_id(p) for p in peers])
    rows, cols = x_ref.shape
    if by_column:
        mine = out_ref.at[:, pl.ds(pl.multiple_of(me * cols, cols), cols)]
    else:
        mine = out_ref.at[pl.ds(pl.multiple_of(me * rows, rows), rows), :]
    copies = [
        pltpu.make_async_remote_copy(
            src_ref=x_ref,
            dst_ref=mine,
            send_sem=send.at[i],
            recv_sem=recv.at[i],
            device_id=mp_id(p),
            device_id_type=MESH,
        )
        for i, p in enumerate(peers)
    ]
    for copy in copies:
        copy.start()
    own = pltpu.make_async_copy(x_ref, mine, local)
    own.start()
    own.wait()
    for copy in copies:
        copy.wait()


def gather_mp(x, n, by_column, cid):
    rows, cols = x.shape
    shape = (rows, cols * n) if by_column else (rows * n, cols)
    return pl.pallas_call(
        functools.partial(gather_mp_kernel, n, by_column),
        out_shape=sds(shape, x.dtype),
        in_specs=[VM],
        out_specs=VM,
        scratch_shapes=[
            pltpu.SemaphoreType.DMA((n - 1,)),
            pltpu.SemaphoreType.DMA((n - 1,)),
            pltpu.SemaphoreType.DMA,
        ],
        compiler_params=params(collective_id=cid, has_side_effects=True),
        name="gather_mp",
    )(x)


def scatter_mp_kernel(n, gated_ref, w_ref, feat_ref, out_ref, unit_ref, staged, landed, send, recv):
    me = lax.axis_index("mp")
    peers = [lax.rem(me + k, n) for k in range(1, n)]
    quarter = out_ref.shape[0]

    def block(m):
        rows = pl.ds(pl.multiple_of(m * quarter, quarter), quarter)
        return jnp.dot(gated_ref[rows, :], w_ref[...], preferred_element_type=F32)

    enter([mp_id(p) for p in peers])
    for i, p in enumerate(peers):
        staged[i] = block(p).astype(BF16)
    copies = [
        pltpu.make_async_remote_copy(
            src_ref=staged.at[i],
            dst_ref=landed.at[i],
            send_sem=send.at[i],
            recv_sem=recv.at[i],
            device_id=mp_id(p),
            device_id_type=MESH,
        )
        for i, p in enumerate(peers)
    ]
    for copy in copies:
        copy.start()
    mine = pl.ds(pl.multiple_of(me * quarter, quarter), quarter)
    total = block(me) + feat_ref[mine, :].astype(F32)
    for i, copy in enumerate(copies):
        copy.wait()
        total = total + landed[i].astype(F32)
    out_ref[...] = total
    inv = 1.0 / jnp.sqrt(jnp.sum(total * total, axis=-1, keepdims=True) + epsilon_unit)
    unit_ref[...] = (total * inv).astype(BF16)


def scatter_mp(gated, w_out, features, n, cid):
    rows, width = features.shape
    quarter = rows // n
    return pl.pallas_call(
        functools.partial(scatter_mp_kernel, n),
        out_shape=(sds((quarter, width), F32), sds((quarter, width), BF16)),
        in_specs=[VM] * 3,
        out_specs=(VM,) * 2,
        scratch_shapes=[
            pltpu.VMEM((n - 1, quarter, width), BF16),
            pltpu.VMEM((n - 1, quarter, width), BF16),
            pltpu.SemaphoreType.DMA((n - 1,)),
            pltpu.SemaphoreType.DMA((n - 1,)),
        ],
        compiler_params=params(collective_id=cid, has_side_effects=True),
        name="scatter_mp",
    )(gated, w_out, features)


def weights_kernel(
    nx, nz, x_ref, out_ref, stage_x, stage_z, land_c, land_x, land_z,
    send_c, recv_c, send_x, recv_x, send_z, recv_z,
):
    ix, iz, ic, im = (lax.axis_index(a) for a in ("x", "z", "c", "mp"))
    peer_c = (ix, iz, 1 - ic, im)
    xs = [lax.rem(ix + k, nx) for k in range(1, nx)]
    zs = [lax.rem(iz + k, nz) for k in range(1, nz)]
    peers_x = [(p, iz, ic, im) for p in xs]
    peers_z = [(ix, p, ic, im) for p in zs]
    enter([peer_c] + peers_x + peers_z)
    first = pltpu.make_async_remote_copy(
        src_ref=x_ref.at[:, :, :, 1 - ic],
        dst_ref=land_c,
        send_sem=send_c,
        recv_sem=recv_c,
        device_id=peer_c,
        device_id_type=MESH,
    )
    first.start()
    first.wait()
    copies = []
    for i, p in enumerate(xs):
        stage_x[i] = (x_ref[:, p, :, ic].astype(F32) + land_c[:, p].astype(F32)).astype(BF16)
        copies.append(
            pltpu.make_async_remote_copy(
                src_ref=stage_x.at[i],
                dst_ref=land_x.at[i],
                send_sem=send_x.at[i],
                recv_sem=recv_x.at[i],
                device_id=peers_x[i],
                device_id_type=MESH,
            )
        )
        copies[-1].start()
    total = x_ref[:, ix, :, ic].astype(F32) + land_c[:, ix].astype(F32)
    for i, copy in enumerate(copies):
        copy.wait()
        total = total + land_x[i].astype(F32)
    stage_z[...] = total.astype(BF16)
    copies = []
    for i, p in enumerate(zs):
        copies.append(
            pltpu.make_async_remote_copy(
                src_ref=stage_z.at[:, p],
                dst_ref=land_z.at[i],
                send_sem=send_z.at[i],
                recv_sem=recv_z.at[i],
                device_id=peers_z[i],
                device_id_type=MESH,
            )
        )
        copies[-1].start()
    result = stage_z[:, iz].astype(F32)
    for i, copy in enumerate(copies):
        copy.wait()
        result = result + land_z[i].astype(F32)
    out_ref[...] = result


def reduce_weights(parts, cid):
    groups, nx, nz, nc, rows, cols = parts.shape
    dma = pltpu.SemaphoreType.DMA
    return pl.pallas_call(
        functools.partial(weights_kernel, nx, nz),
        out_shape=sds((groups, rows, cols), F32),
        in_specs=[VM],
        out_specs=VM,
        scratch_shapes=[
            pltpu.VMEM((nx - 1, groups, nz, rows, cols), BF16),
            pltpu.VMEM((groups, nz, rows, cols), BF16),
            pltpu.VMEM((groups, nx, nz, rows, cols), BF16),
            pltpu.VMEM((nx - 1, groups, nz, rows, cols), BF16),
            pltpu.VMEM((nz - 1, groups, rows, cols), BF16),
            dma, dma, dma((nx - 1,)), dma((nx - 1,)), dma((nz - 1,)), dma((nz - 1,)),
        ],
        compiler_params=params(collective_id=cid, has_side_effects=True),
        name="reduce_weights",
    )(parts)


def normalize(rows_in):
    centered = rows_in - jnp.mean(rows_in, axis=-1, keepdims=True)
    spread = jnp.mean(centered * centered, axis=-1, keepdims=True)
    return centered / jnp.sqrt(spread + epsilon_norm)


def attend(projected, length_here):
    gating = projected[0]
    values = projected[1]
    queries = projected[2]
    key_rows = projected[3]
    steps_n = projected.shape[1]
    scores = jnp.einsum(
        "thd,shd->hts", queries, key_rows, preferred_element_type=jnp.float32
    ) / jnp.sqrt(jnp.float32(projected.shape[3]))
    places = jnp.arange(steps_n, dtype=jnp.int32)
    allowed = (places[None, :] <= places[:, None]) & (places[None, :] < length_here)
    weights = jnp.where(
        allowed[None], jax.nn.silu(scores) / length_here.astype(jnp.float32), 0.0
    ).astype(jnp.bfloat16)
    mixed_out = jnp.einsum("hts,shd->thd", weights, values, preferred_element_type=jnp.float32)
    return (normalize(mixed_out) * gating.astype(jnp.float32)).astype(jnp.bfloat16)


def silu_slope(preact):
    sigma = jax.nn.sigmoid(preact)
    return sigma * (1.0 + preact * (1.0 - sigma))


ALL = ("x", "z", "c", "mp")
DP = ("x", "z", "c")


def exchange(x, axes):
    return lax.all_to_all(x, axes, split_axis=0, concat_axis=0, tiled=True)


def per_device(history, lengths, source, owners, item_rows, catalogue, w_in, w_out):
    nx, nz, nc, mp_count = (lax.axis_size(a) for a in ALL)
    dp_count = nx * nz * nc
    dev_count = dp_count * mp_count
    here_dp = (lax.axis_index("x") * nz + lax.axis_index("z")) * nc + lax.axis_index("c")
    here_mp = lax.axis_index("mp")
    seq_dev, steps_n, cols_here = history.shape
    seq_total = source.shape[0]
    rows_all = seq_dev * steps_n
    quarter = rows_all // mp_count
    width = catalogue.shape[1]

    want, chosen, rank, col = slots(owners.T, item_rows.T, dev_count)
    asked = exchange(want.reshape(dev_count, 1, 128), ALL).reshape(dev_count, 128)

    slot_ids = jnp.arange(seq_dev, dtype=jnp.int32)
    my_seqs = here_dp * seq_dev + slot_ids
    places = jnp.arange(seq_total, dtype=jnp.int32)
    target = jnp.sum(jnp.where(source[None, :] == my_seqs[:, None], places[None, :], 0), axis=1)
    dest_dev = target // seq_dev
    dests = jnp.arange(dp_count, dtype=jnp.int32)
    seq_for = jnp.sum(jnp.where(dest_dev[None, :] == dests[:, None], slot_ids[None, :], 0), axis=1)
    taken = lax.dynamic_slice_in_dim(source, here_dp * seq_dev, seq_dev, 0)
    counts = jnp.sum(jnp.where(places[None, :] == taken[:, None], lengths[None, :], 0), axis=1)
    arrived = exchange(pick_blocks(seq_for, history), DP)
    local_rows = pick_blocks(taken // seq_dev, arrived).reshape(rows_all, cols_here)

    tiles = catalogue.reshape(catalogue.shape[0], width // 128, 128)
    fetched = exchange(gather_rows(asked, tiles), ALL)

    flat_rows = gather_mp(local_rows, mp_count, True, 1)
    normed = normalize(flat_rows.astype(jnp.float32)).astype(jnp.bfloat16)
    preact = jnp.einsum("rd,cdh->crh", normed, w_in, preferred_element_type=jnp.float32)
    projected = jax.nn.silu(preact).astype(jnp.bfloat16)
    cols_heads = w_in.shape[2]
    heads_here = cols_heads // DH
    grouped = projected.reshape(4, seq_dev, steps_n, heads_here, DH)

    def run_all(inputs):
        return jax.vmap(attend, in_axes=(1, 0))(inputs, counts)

    gated, back = jax.vjp(run_all, grouped)
    gated_flat = gated.reshape(rows_all, cols_heads)
    out_rows, unit_rows = scatter_mp(gated_flat, w_out, flat_rows, mp_count, 2)
    unit_tiles = unit_rows.reshape(quarter, width // 128, 128)
    units = gather_rows(chosen, unit_tiles)
    fetched, units = lax.optimization_barrier((fetched, units))
    landed = exchange(units, ALL)

    position = here_mp * quarter + jnp.arange(quarter, dtype=jnp.int32)
    count_of = jnp.sum(
        jnp.where((position // steps_n)[:, None] == slot_ids[None, :], counts[None, :], 0), axis=1
    )
    valid = jnp.broadcast_to((position % steps_n < count_of).astype(F32)[None, :], (8, quarter))
    out_grad, coef = loss_call(fetched, out_rows, rank, col, valid)
    coefs = exchange(coef.reshape(dev_count, 1, 128), ALL).reshape(dev_count, 128)

    out_cotangent = gather_mp(out_grad, mp_count, False, 3)
    w_out_part = jnp.einsum(
        "rd,rh->dh", out_cotangent, gated_flat, preferred_element_type=jnp.float32
    )
    gated_cotangent = jnp.einsum(
        "rd,hd->rh", out_cotangent, w_out, preferred_element_type=jnp.float32
    ).astype(jnp.bfloat16)
    (grouped_cotangent,) = back(gated_cotangent.reshape(seq_dev, steps_n, heads_here, DH))
    projected_cotangent = grouped_cotangent.reshape(4, rows_all, cols_heads)
    preact_cotangent = (projected_cotangent.astype(jnp.float32) * silu_slope(preact)).astype(
        jnp.bfloat16
    )
    w_in_part = jnp.einsum(
        "rd,crh->cdh", normed, preact_cotangent, preferred_element_type=jnp.float32
    )
    parts = jnp.concatenate([w_in_part.astype(BF16), w_out_part.astype(BF16)[None]], axis=0)
    rows_out = width // dp_count
    sums = reduce_weights(parts.reshape(5, nx, nz, nc, rows_out, cols_heads), 4)
    cat_grad = catalogue_call(landed, asked, coefs, catalogue)
    return (sums[:4], sums[4].T, cat_grad)


def solution(mesh):
    split = Mesh(mesh.devices.reshape(4, 8, 2, 4), ALL)
    placed = (
        P(DP, None, "mp"),
        P(),
        P(),
        P(ALL, None),
        P(ALL, None),
        P(ALL, None),
        P(None, None, "mp"),
        P("mp", None),
    )
    return jax.shard_map(
        per_device,
        mesh=split,
        in_specs=placed,
        out_specs=(P(None, DP, "mp"), P("mp", DP), P(ALL, None)),
        check_vma=False,
    )
```

```python
import functools

import jax
import jax.numpy as jnp
from jax import lax
from jax.experimental import pallas as pl
from jax.experimental.pallas import tpu as pltpu
from jax.sharding import Mesh, PartitionSpec as P

DH = 128
CAP = 6
MESH = pl.DeviceIdType.MESH
F32 = jnp.float32
BF16 = jnp.bfloat16

cosine_divisor = 0.05
epsilon_norm = 1e-05
epsilon_unit = 1e-06

VM = pl.BlockSpec(memory_space=pltpu.VMEM)
SM = pl.BlockSpec(memory_space=pltpu.SMEM)


def sds(shape, dtype):
    return jax.ShapeDtypeStruct(shape, dtype)


def params(**kw):
    return pltpu.CompilerParams(vmem_limit_bytes=60 * 1024 * 1024, **kw)


def slots_kernel(own_ref, row_ref, want_ref, event_ref, rank_ref, col_ref):
    owners_n, events = rank_ref.shape
    who = lax.broadcasted_iota(jnp.int32, (owners_n, events), 0)
    named = jnp.zeros((owners_n, events), F32)
    rows = jnp.zeros((owners_n, events), jnp.int32)
    cols = jnp.zeros((owners_n, events), jnp.int32)
    for j in range(own_ref.shape[0]):
        mask = own_ref[j : j + 1, :] == who
        named = jnp.where(mask, 1.0, named)
        rows = jnp.where(mask, row_ref[j : j + 1, :], rows)
        cols = jnp.where(mask, j, cols)
    before = (
        lax.broadcasted_iota(jnp.int32, (events, events), 0)
        < lax.broadcasted_iota(jnp.int32, (events, events), 1)
    ).astype(F32)
    rank = jnp.dot(
        named.astype(BF16), before.astype(BF16), preferred_element_type=F32
    ).astype(jnp.int32)
    rank = jnp.where(named > 0.0, rank, -1)
    rank_ref[...] = rank
    col_ref[...] = cols
    event = lax.broadcasted_iota(jnp.int32, (owners_n, events), 1)
    lane = lax.broadcasted_iota(jnp.int32, want_ref.shape, 1)
    want = jnp.full(want_ref.shape, -1, jnp.int32)
    chosen = jnp.zeros(want_ref.shape, jnp.int32)
    for r in range(CAP):
        here = rank == r
        row_r = jnp.max(jnp.where(here, rows, -1), axis=1, keepdims=True)
        event_r = jnp.max(jnp.where(here, event, 0), axis=1, keepdims=True)
        want = jnp.where(lane == r, row_r, want)
        chosen = jnp.where(lane == r, event_r, chosen)
    want_ref[...] = want
    event_ref[...] = chosen


OVER_ROWS = (((0,), (0,)), ((), ()))
OVER_COLS = (((1,), (1,)), ((), ()))


def sigmoid(v):
    return 1.0 / (1.0 + jnp.exp(-v))


def silu_slope(v):
    s = sigmoid(v)
    return s * (1.0 + v * (1.0 - s))


def center(v):
    moved = v - jnp.mean(v, axis=-1, keepdims=True)
    inv = 1.0 / jnp.sqrt(jnp.mean(moved * moved, axis=-1, keepdims=True) + epsilon_norm)
    return moved * inv, inv


def attention_weights(q, k, count):
    n = q.shape[0]
    scores = lax.dot_general(q, k, OVER_COLS, preferred_element_type=F32) * (DH**-0.5)
    t = lax.broadcasted_iota(jnp.int32, (n, n), 0)
    s = lax.broadcasted_iota(jnp.int32, (n, n), 1)
    first = t - lax.rem(t, STEPS)
    mask = (s >= first) & (s <= t) & ((s - first).astype(F32) < count)
    return scores, mask


STEPS = 32


def step_kernel(
    seq_for, anchors, owners_ref, rows_ref, count_ref, valid_ref,
    history_hbm, tiles_hbm, cat_hbm, w_in_hbm, w_out_hbm,
    cat_grad_ref, sums_ref,
    hist, hist_out, arrived, tiles, cat, w_in, w_out, load_sem,
    want, event, rank, col, chosen_v, want_out, asked, asked_s, chosen_s, small_sem,
    fetch_out, fetch_in, unit_out, unit_in, coef_out, coef_in,
    part, flat, normed, preact, proj, gated, staged, landed,
    out_rows, tall, mat, cosine, expo, grad, cot, gated_cot, pre_cot,
    parts, land_c, stage_x, land_x, stage_z, land_z, hot, side,
    ids_sem, hist_sem, fetch_sem, unit_sem, coef_sem, gat_sem, sca_sem, cot_sem,
    c_sem, x_sem, z_sem,
):
    ix, iz, ic, im = (lax.axis_index(a) for a in ALL)
    nx, nz, nc, nm = NX, NZ, NC, NM
    n = nx * nz * nc * nm
    here_dp = (ix * nz + iz) * nc + ic
    me = here_dp * nm + im
    n_dp = nx * nz * nc

    def dp_at(d):
        return (lax.div(d, nz * nc), lax.rem(lax.div(d, nc), nz), lax.rem(d, nc))

    def device(d):
        return dp_at(lax.div(d, nm)) + (lax.rem(d, nm),)

    loads = [
        pltpu.make_async_copy(a, b, load_sem.at[i])
        for i, (a, b) in enumerate(
            [(history_hbm, hist), (tiles_hbm, tiles), (w_in_hbm, w_in), (w_out_hbm, w_out), (cat_hbm, cat)]
        )
    ]
    for load in loads:
        load.start()

    barrier = pltpu.get_barrier_semaphore()

    def greet(k, carry):
        pl.semaphore_signal(
            barrier, inc=1, device_id=device(lax.rem(me + k, n)), device_id_type=MESH
        )
        return carry

    lax.fori_loop(1, n, greet, 0)

    slots_kernel(owners_ref, rows_ref, want, event, rank, col)
    want_out[...] = want[...].reshape(want_out.shape)
    chosen_v[...] = event[...].reshape(chosen_v.shape)
    to_smem = pltpu.make_async_copy(chosen_v, chosen_s, small_sem.at[0])
    to_smem.start()
    loads[0].wait()

    def stage(d, carry):
        hist_out[d] = hist[seq_for[d]]
        return carry

    lax.fori_loop(0, n_dp, stage, 0, unroll=4)
    pl.semaphore_wait(barrier, n - 1)

    def send_all(src, dst, sems, first=1, last=n):
        def one(k, carry):
            d = lax.rem(me + k, n)
            push(src, dst, sems, d)
            return carry

        lax.fori_loop(first, last, one, 0)

    def push(src, dst, sems, d):
        pltpu.make_async_remote_copy(
            src_ref=src.at[d],
            dst_ref=dst.at[me],
            send_sem=sems.at[0],
            recv_sem=sems.at[1],
            device_id=device(d),
            device_id_type=MESH,
        ).start()

    def finish(ref, sems, which, count):
        block = ref.at[pl.ds(0, count)]
        pltpu.make_async_copy(block, block, sems.at[which]).wait()

    send_all(want_out, asked, ids_sem)
    asked[me] = want_out[me]

    def send_history(k, carry):
        d = lax.rem(here_dp + k, n_dp)
        pltpu.make_async_remote_copy(
            src_ref=hist_out.at[d],
            dst_ref=arrived.at[here_dp],
            send_sem=hist_sem.at[0],
            recv_sem=hist_sem.at[1],
            device_id=dp_at(d) + (im,),
            device_id_type=MESH,
        ).start()
        return carry

    lax.fori_loop(1, n_dp, send_history, 0)
    arrived[here_dp] = hist_out[here_dp]

    loads[1].wait()
    to_smem.wait()
    finish(asked, ids_sem, 1, n - 1)
    to_smem = pltpu.make_async_copy(asked, asked_s, small_sem.at[1])
    to_smem.start()
    to_smem.wait()

    def fill(out, at, d, table, idx):
        for r in range(CAP):
            out[at, r] = table[jnp.maximum(idx[d, 0, r], 0)]

    def serve(out, into, table, idx, sems, first=1, last=n):
        d0 = lax.rem(me + first, n)
        fill(out, d0, d0, table, idx)

        def one(k, carry):
            d = lax.rem(me + k, n)
            fill(out, d, d, table, idx)
            push(out, into, sems, lax.rem(me + k - 1, n))
            return carry

        lax.fori_loop(first + 1, last, one, 0)
        push(out, into, sems, lax.rem(me + last - 1, n))

    serve(fetch_out, fetch_in, tiles, asked_s, fetch_sem)
    fill(fetch_in, me, me, tiles, asked_s)

    peers = [lax.rem(im + k, nm) for k in range(1, nm)]
    finish(arrived, hist_sem, 1, n_dp - 1)
    for s in range(anchors.shape[0]):
        part[s * STEPS : (s + 1) * STEPS, :] = arrived[anchors[s]]
    rows_all, cols_here = part.shape
    width = flat.shape[1]
    quarter = rows_all // nm
    mine = pl.ds(pl.multiple_of(im * cols_here, cols_here), cols_here)
    gathers = [
        pltpu.make_async_remote_copy(
            src_ref=part,
            dst_ref=flat.at[:, mine],
            send_sem=gat_sem.at[0, i],
            recv_sem=gat_sem.at[1, i],
            device_id=(ix, iz, ic, p),
            device_id_type=MESH,
        )
        for i, p in enumerate(peers)
    ]
    for copy in gathers:
        copy.start()
    flat[:, mine] = part[...]
    for copy in gathers:
        copy.wait()

    loads[2].wait()
    loads[3].wait()
    for b in range(nm):
        rows = slice(b * quarter, (b + 1) * quarter)
        scaled, _ = center(flat[rows, :].astype(F32))
        normed[rows, :] = scaled.astype(BF16)
    heads = cols_here // DH
    for c in range(4):
        z = jnp.dot(normed[...], w_in[c], preferred_element_type=F32)
        preact[c] = z
        proj[c] = (z * sigmoid(z)).astype(BF16)

    def forward(rows, cols):
        count = count_ref[rows, :]
        scores, mask = attention_weights(proj[2, rows, cols], proj[3, rows, cols], count)
        weights = jnp.where(mask, scores * sigmoid(scores) / count, 0.0).astype(BF16)
        mixed = jnp.dot(weights, proj[1, rows, cols], preferred_element_type=F32)
        scaled, inv = center(mixed)
        return scores, mask, weights, scaled, inv

    for b in range(nm):
        for h in range(heads):
            rows = slice(b * quarter, (b + 1) * quarter)
            cols = slice(h * DH, (h + 1) * DH)
            scaled = forward(rows, cols)[3]
            gated[rows, cols] = (scaled * proj[0, rows, cols].astype(F32)).astype(BF16)

    def block(m):
        rows = pl.ds(pl.multiple_of(m * quarter, quarter), quarter)
        return jnp.dot(gated[rows, :], w_out[...], preferred_element_type=F32)

    for i, p in enumerate(peers):
        staged[i] = block(p).astype(BF16)
    copies = [
        pltpu.make_async_remote_copy(
            src_ref=staged.at[i],
            dst_ref=landed.at[i],
            send_sem=sca_sem.at[0, i],
            recv_sem=sca_sem.at[1, i],
            device_id=(ix, iz, ic, p),
            device_id_type=MESH,
        )
        for i, p in enumerate(peers)
    ]
    for copy in copies:
        copy.start()
    own = pl.ds(pl.multiple_of(im * quarter, quarter), quarter)
    total = block(im) + flat[own, :].astype(F32)
    for i, copy in enumerate(copies):
        copy.wait()
        total = total + landed[i].astype(F32)
    out_rows[...] = total
    inv_out = 1.0 / jnp.sqrt(jnp.sum(total * total, axis=-1, keepdims=True) + epsilon_unit)
    unit = total * inv_out
    unit_b = unit.astype(BF16)

    chunks, lanes = width // 128, 128
    for c in range(chunks):
        tall[pl.ds(c, quarter, stride=chunks), :] = unit[:, c * lanes : (c + 1) * lanes]
    unit_tiles = tiles.at[pl.ds(0, quarter)]
    unit_tiles[...] = tall[0 : quarter * chunks, :].reshape(quarter, chunks, lanes).astype(BF16)
    serve(unit_out, unit_in, unit_tiles, chosen_s, unit_sem)
    fill(unit_in, me, me, unit_tiles, chosen_s)

    finish(fetch_in, fetch_sem, 1, n - 1)

    def spread(ref, r):
        tall[...] = ref[:, r].astype(F32).reshape(n * chunks, lanes)

    ranks = rank[...]
    sums = jnp.zeros((1, quarter), F32)
    inverse = []
    for r in range(CAP):
        spread(fetch_in, r)
        squares = jnp.zeros((n, lanes), F32)
        for c in range(chunks):
            chunk = tall[pl.ds(c, n, stride=chunks), :]
            squares = squares + chunk * chunk
            mat[r * n : (r + 1) * n, c * lanes : (c + 1) * lanes] = chunk.astype(BF16)
        inv = 1.0 / jnp.sqrt(jnp.sum(squares, axis=-1, keepdims=True) + epsilon_unit)
        inverse.append(inv)
        dots = lax.dot_general(
            mat[r * n : (r + 1) * n, :], unit_b, OVER_COLS, preferred_element_type=F32
        )
        cos = dots * inv
        ex = jnp.where(ranks == r, jnp.exp(cos / cosine_divisor), 0.0)
        cosine[r] = cos
        expo[r] = ex
        sums = sums + jnp.sum(ex, axis=0, keepdims=True)
    valid = valid_ref[0:1, :]
    scale = valid / sums
    first = (col[...] == 0).astype(F32) * valid
    lane = lax.broadcasted_iota(jnp.int32, (n, lanes), 1)
    coef = jnp.zeros((n, lanes), F32)
    slope = jnp.zeros((quarter, width), F32)
    for r in range(CAP):
        share = expo[r] * scale - jnp.where(ranks == r, first, 0.0)
        weight = share * (inverse[r] / cosine_divisor)
        slope = slope + lax.dot_general(
            weight.astype(BF16), mat[r * n : (r + 1) * n, :], OVER_ROWS, preferred_element_type=F32
        )
        a = jnp.sum(weight, axis=-1, keepdims=True)
        b = jnp.sum(weight * cosine[r], axis=-1, keepdims=True) * inverse[r]
        coef = jnp.where(lane == r, a, coef)
        coef = jnp.where(lane == r + 8, b, coef)
    along = jnp.sum(unit * slope, axis=-1, keepdims=True)
    grad[...] = ((slope - unit * along) * inv_out).astype(BF16)
    coef_out[...] = coef.reshape(coef_out.shape)
    copies = [
        pltpu.make_async_remote_copy(
            src_ref=grad,
            dst_ref=cot.at[own, :],
            send_sem=cot_sem.at[0, i],
            recv_sem=cot_sem.at[1, i],
            device_id=(ix, iz, ic, p),
            device_id_type=MESH,
        )
        for i, p in enumerate(peers)
    ]
    for copy in copies:
        copy.start()
    send_all(coef_out, coef_in, coef_sem)
    coef_in[me] = coef_out[me]
    cot[own, :] = grad[...]
    for copy in copies:
        copy.wait()

    gated_cot[...] = lax.dot_general(
        cot[...], w_out[...], OVER_COLS, preferred_element_type=F32
    ).astype(BF16)
    for b in range(nm):
        for h in range(heads):
            rows = slice(b * quarter, (b + 1) * quarter)
            cols = slice(h * DH, (h + 1) * DH)
            count = count_ref[rows, :]
            scores, mask, weights, scaled, inv = forward(rows, cols)
            gc = gated_cot[rows, cols].astype(F32)
            d_gating = gc * scaled
            d_scaled = gc * proj[0, rows, cols].astype(F32)
            d_mixed = inv * (
                d_scaled
                - jnp.mean(d_scaled, axis=-1, keepdims=True)
                - scaled * jnp.mean(d_scaled * scaled, axis=-1, keepdims=True)
            )
            d_mixed = d_mixed.astype(BF16)
            d_weights = lax.dot_general(
                d_mixed, proj[1, rows, cols], OVER_COLS, preferred_element_type=F32
            )
            d_weights = d_weights.astype(BF16).astype(F32)
            d_values = lax.dot_general(weights, d_mixed, OVER_ROWS, preferred_element_type=F32)
            d_scores = jnp.where(
                mask, d_weights * silu_slope(scores) * (DH**-0.5) / count, 0.0
            ).astype(BF16)
            d_queries = jnp.dot(d_scores, proj[3, rows, cols], preferred_element_type=F32)
            d_keys = lax.dot_general(
                d_scores, proj[2, rows, cols], OVER_ROWS, preferred_element_type=F32
            )
            for c, d in enumerate((d_gating, d_values, d_queries, d_keys)):
                at = slice(c * cols_here + h * DH, c * cols_here + (h + 1) * DH)
                pre_cot[rows, at] = (
                    d.astype(BF16).astype(F32) * silu_slope(preact[c, rows, cols])
                ).astype(BF16)

    block_rows = width // nx
    groups = parts.shape[0]
    peer_c = (ix, iz, 1 - ic, im)
    swaps = []
    order = [lax.rem(ix + k, nx) for k in list(range(1, nx)) + [0]]
    for i, p in enumerate(order):
        at = pl.ds(pl.multiple_of(p * block_rows, block_rows), block_rows)
        res = lax.dot_general(normed[:, at], pre_cot[...], OVER_ROWS, preferred_element_type=F32)
        for c in range(4):
            parts[c, p] = (
                res[:, c * cols_here : (c + 1) * cols_here].astype(BF16).reshape(parts.shape[2:])
            )
        res = lax.dot_general(cot[:, at], gated[...], OVER_ROWS, preferred_element_type=F32)
        parts[4, p] = res.astype(BF16).reshape(parts.shape[2:])
        swaps.append(
            pltpu.make_async_remote_copy(
                src_ref=parts.at[:, p, :, 1 - ic],
                dst_ref=land_c.at[:, p],
                send_sem=c_sem.at[0, i],
                recv_sem=c_sem.at[1, i],
                device_id=peer_c,
                device_id_type=MESH,
            )
        )
        swaps[-1].start()
    copies = []
    for i in range(nx - 1):
        p = order[i]
        swaps[i].wait()
        stage_x[i] = (parts[:, p, :, ic].astype(F32) + land_c[:, p].astype(F32)).astype(BF16)
        copies.append(
            pltpu.make_async_remote_copy(
                src_ref=stage_x.at[i],
                dst_ref=land_x.at[i],
                send_sem=x_sem.at[0, i],
                recv_sem=x_sem.at[1, i],
                device_id=(p, iz, ic, im),
                device_id_type=MESH,
            )
        )
        copies[-1].start()
    swaps[nx - 1].wait()
    held = parts[:, ix, :, ic].astype(F32) + land_c[:, ix].astype(F32)
    for i, copy in enumerate(copies):
        copy.wait()
        held = held + land_x[i].astype(F32)
    stage_z[...] = held.astype(BF16)
    copies = []
    for i in range(nz - 1):
        p = lax.rem(iz + 1 + i, nz)
        copies.append(
            pltpu.make_async_remote_copy(
                src_ref=stage_z.at[:, p],
                dst_ref=land_z.at[i],
                send_sem=z_sem.at[0, i],
                recv_sem=z_sem.at[1, i],
                device_id=(ix, p, ic, im),
                device_id_type=MESH,
            )
        )
        copies[-1].start()
    held = stage_z[:, iz].astype(F32)
    for i, copy in enumerate(copies):
        copy.wait()
        held = held + land_z[i].astype(F32)
    sums_ref[...] = held

    loads[4].wait()
    finish(coef_in, coef_sem, 1, n - 1)
    finish(unit_in, unit_sem, 1, n - 1)
    wanted = asked[...].reshape(n, lanes)
    coef = coef_in[...].reshape(n, lanes)
    rows_cat = cat.shape[0]
    row = lax.broadcasted_iota(jnp.int32, (n, rows_cat), 1)
    for r in range(CAP):
        spread(unit_in, r)
        a = coef[:, r : r + 1]
        b = coef[:, r + 8 : r + 9]
        high = b.astype(BF16).astype(F32)
        span = slice(r * n, (r + 1) * n)
        for c in range(chunks):
            chunk = tall[pl.ds(c, n, stride=chunks), :]
            mat[span, c * lanes : (c + 1) * lanes] = (chunk * a).astype(BF16)
        side[span, :] = jnp.where(
            lane == 0, high, jnp.where(lane == 1, b - high, 0.0)
        ).astype(BF16)
        hot[span, :] = (wanted[:, r : r + 1] == row).astype(F32).astype(BF16)
    both = lax.dot_general(hot[...], side[...], OVER_ROWS, preferred_element_type=F32)
    b_row = both[:, 0:1] + both[:, 1:2]
    for c in range(0, width, 256):
        res = lax.dot_general(hot[...], mat[:, c : c + 256], OVER_ROWS, preferred_element_type=F32)
        cat_grad_ref[:, c : c + 256] = res - b_row * cat[:, c : c + 256].astype(F32)

    finish(want_out, ids_sem, 0, n - 1)
    finish(hist_out, hist_sem, 0, n_dp - 1)
    finish(fetch_out, fetch_sem, 0, n - 1)
    finish(unit_out, unit_sem, 0, n - 1)
    finish(coef_out, coef_sem, 0, n - 1)


ALL = ("x", "z", "c", "mp")
DP = ("x", "z", "c")
NX, NZ, NC, NM = 4, 8, 2, 4


def step(seq_for, anchors, owners_t, rows_t, counts, valid, history, tiles, catalogue, w_in, w_out):
    n_dp = NX * NZ * NC
    n = n_dp * NM
    seqs, steps, cols = history.shape
    rows_all = seqs * steps
    rows_cat, width = catalogue.shape
    quarter = rows_all // NM
    chunks = width // 128
    rows_out = width // n_dp
    dma = pltpu.SemaphoreType.DMA
    V = pltpu.VMEM
    I32 = jnp.int32
    anyw = pl.BlockSpec(memory_space=pl.ANY)
    message = (n, CAP, chunks, 128)
    scratch = [
        V(history.shape, BF16), V((n_dp, steps, cols), BF16), V((n_dp, steps, cols), BF16),
        V(tiles.shape, BF16), V(catalogue.shape, BF16), V(w_in.shape, BF16), V(w_out.shape, BF16), dma((5,)),
        V((n, 128), I32), V((n, 128), I32), V((n, quarter), I32), V((n, quarter), I32),
        V((n, 1, 128), I32), V((n, 1, 128), I32), V((n, 1, 128), I32),
        pltpu.SMEM((n, 1, 128), I32), pltpu.SMEM((n, 1, 128), I32), dma((2,)),
        V(message, BF16), V(message, BF16), V(message, BF16), V(message, BF16),
        V((n, 1, 128), F32), V((n, 1, 128), F32),
        V((rows_all, cols), BF16), V((rows_all, width), BF16), V((rows_all, width), BF16),
        V((4, rows_all, cols), F32), V((4, rows_all, cols), BF16), V((rows_all, cols), BF16),
        V((NM - 1, quarter, width), BF16), V((NM - 1, quarter, width), BF16),
        V((quarter, width), F32), V((n * chunks, 128), F32), V((CAP * n, width), BF16),
        V((CAP, n, quarter), F32), V((CAP, n, quarter), F32), V((quarter, width), BF16),
        V((rows_all, width), BF16), V((rows_all, cols), BF16), V((rows_all, 4 * cols), BF16),
        V((5, NX, NZ, NC, rows_out, cols), BF16), V((5, NX, NZ, rows_out, cols), BF16),
        V((NX - 1, 5, NZ, rows_out, cols), BF16), V((NX - 1, 5, NZ, rows_out, cols), BF16),
        V((5, NZ, rows_out, cols), BF16), V((NZ - 1, 5, rows_out, cols), BF16),
        V((CAP * n, rows_cat), BF16), V((CAP * n, 128), BF16),
        dma((2,)), dma((2,)), dma((2,)), dma((2,)), dma((2,)),
        dma((2, NM - 1)), dma((2, NM - 1)), dma((2, NM - 1)),
        dma((2, NX)), dma((2, NX - 1)), dma((2, NZ - 1)),
    ]
    return pl.pallas_call(
        step_kernel,
        out_shape=(sds((rows_cat, width), F32), sds((5, rows_out, cols), F32)),
        in_specs=[SM, SM, VM, VM, VM, VM] + [anyw] * 5,
        out_specs=(VM, VM),
        scratch_shapes=scratch,
        compiler_params=params(collective_id=0, has_side_effects=True),
        name="step",
    )(seq_for, anchors, owners_t, rows_t, counts, valid, history, tiles, catalogue, w_in, w_out)


def per_device(history, lengths, source, owners, item_rows, catalogue, w_in, w_out):
    n_dp = NX * NZ * NC
    here_dp = (lax.axis_index("x") * NZ + lax.axis_index("z")) * NC + lax.axis_index("c")
    here_mp = lax.axis_index("mp")
    seq_dev, steps_n, _ = history.shape
    seq_total = source.shape[0]
    rows_all = seq_dev * steps_n
    quarter = rows_all // NM

    slot_ids = jnp.arange(seq_dev, dtype=jnp.int32)
    my_seqs = here_dp * seq_dev + slot_ids
    places = jnp.arange(seq_total, dtype=jnp.int32)
    target = jnp.sum(jnp.where(source[None, :] == my_seqs[:, None], places[None, :], 0), axis=1)
    dests = jnp.arange(n_dp, dtype=jnp.int32)
    seq_for = jnp.sum(
        jnp.where((target // seq_dev)[None, :] == dests[:, None], slot_ids[None, :], 0), axis=1
    )
    taken = lax.dynamic_slice_in_dim(source, here_dp * seq_dev, seq_dev, 0)
    counts = jnp.sum(jnp.where(places[None, :] == taken[:, None], lengths[None, :], 0), axis=1)
    per_row = jnp.broadcast_to(counts[:, None], (seq_dev, steps_n)).reshape(rows_all)
    spot = jnp.arange(rows_all, dtype=jnp.int32) % steps_n
    valid = lax.dynamic_slice_in_dim((spot < per_row).astype(F32), here_mp * quarter, quarter, 0)
    tiles = catalogue.reshape(catalogue.shape[0], catalogue.shape[1] // 128, 128)
    cat_grad, sums = step(
        seq_for,
        taken // seq_dev,
        owners.T,
        item_rows.T,
        per_row.astype(F32)[:, None],
        jnp.broadcast_to(valid[None, :], (8, quarter)),
        history,
        tiles,
        catalogue,
        w_in,
        w_out,
    )
    return (sums[:4], sums[4].T, cat_grad)


def solution(mesh):
    split = Mesh(mesh.devices.reshape(NX, NZ, NC, NM), ALL)
    placed = (
        P(DP, None, "mp"),
        P(),
        P(),
        P(ALL, None),
        P(ALL, None),
        P(ALL, None),
        P(None, None, "mp"),
        P("mp", None),
    )
    return jax.shard_map(
        per_device,
        mesh=split,
        in_specs=placed,
        out_specs=(P(None, DP, "mp"), P("mp", DP), P(ALL, None)),
        check_vma=False,
    )
```

```python
import functools

import jax
import jax.numpy as jnp
from jax import lax
from jax.experimental import pallas as pl
from jax.experimental.pallas import tpu as pltpu
from jax.sharding import Mesh, PartitionSpec as P

DH = 128
CAP = 6
MESH = pl.DeviceIdType.MESH
F32 = jnp.float32
BF16 = jnp.bfloat16

cosine_divisor = 0.05
epsilon_norm = 1e-05
epsilon_unit = 1e-06

VM = pl.BlockSpec(memory_space=pltpu.VMEM)
SM = pl.BlockSpec(memory_space=pltpu.SMEM)


def sds(shape, dtype):
    return jax.ShapeDtypeStruct(shape, dtype)


def params(**kw):
    return pltpu.CompilerParams(vmem_limit_bytes=60 * 1024 * 1024, **kw)


def slots_kernel(own_ref, row_ref, want_ref, event_ref, rank_ref, col_ref):
    owners_n, events = rank_ref.shape
    who = lax.broadcasted_iota(jnp.int32, (owners_n, events), 0)
    named = jnp.zeros((owners_n, events), F32)
    rows = jnp.zeros((owners_n, events), jnp.int32)
    cols = jnp.zeros((owners_n, events), jnp.int32)
    own = own_ref[...]
    core = lax.rem(lax.div(own, NM), NC)
    own = core * (owners_n // NC) + lax.div(own, NM * NC) * NM + lax.rem(own, NM)
    for j in range(own_ref.shape[0]):
        mask = own[j : j + 1, :] == who
        named = jnp.where(mask, 1.0, named)
        rows = jnp.where(mask, row_ref[j : j + 1, :], rows)
        cols = jnp.where(mask, j, cols)
    before = (
        lax.broadcasted_iota(jnp.int32, (events, events), 0)
        < lax.broadcasted_iota(jnp.int32, (events, events), 1)
    ).astype(F32)
    rank = jnp.dot(
        named.astype(BF16), before.astype(BF16), preferred_element_type=F32
    ).astype(jnp.int32)
    rank = jnp.where(named > 0.0, rank, -1)
    rank_ref[...] = rank
    col_ref[...] = cols
    event = lax.broadcasted_iota(jnp.int32, (owners_n, events), 1)
    lane = lax.broadcasted_iota(jnp.int32, want_ref.shape, 1)
    want = jnp.full(want_ref.shape, -1, jnp.int32)
    chosen = jnp.zeros(want_ref.shape, jnp.int32)
    for r in range(CAP):
        here = rank == r
        row_r = jnp.max(jnp.where(here, rows, -1), axis=1, keepdims=True)
        event_r = jnp.max(jnp.where(here, event, 0), axis=1, keepdims=True)
        want = jnp.where(lane == r, row_r, want)
        chosen = jnp.where(lane == r, event_r, chosen)
    want_ref[...] = want
    event_ref[...] = chosen


OVER_ROWS = (((0,), (0,)), ((), ()))
OVER_COLS = (((1,), (1,)), ((), ()))


def sigmoid(v):
    return 1.0 / (1.0 + jnp.exp(-v))


def silu_slope(v):
    s = sigmoid(v)
    return s * (1.0 + v * (1.0 - s))


def center(v):
    moved = v - jnp.mean(v, axis=-1, keepdims=True)
    inv = 1.0 / jnp.sqrt(jnp.mean(moved * moved, axis=-1, keepdims=True) + epsilon_norm)
    return moved * inv, inv


def attention_weights(q, k, count):
    n = q.shape[0]
    scores = lax.dot_general(q, k, OVER_COLS, preferred_element_type=F32) * (DH**-0.5)
    t = lax.broadcasted_iota(jnp.int32, (n, n), 0)
    s = lax.broadcasted_iota(jnp.int32, (n, n), 1)
    first = t - lax.rem(t, STEPS)
    mask = (s >= first) & (s <= t) & ((s - first).astype(F32) < count)
    return scores, mask


STEPS = 32


def step_kernel(
    source_s, lengths_s, source_ref, owners_ref, rows_ref,
    history_hbm, cat_hbm, w_in_hbm, w_out_hbm,
    cat_grad_ref, sums_ref,
    count_ref, seq_v, seq_s, hist, hist_out, arrived, tiles, cat, w_in, w_out, load_sem,
    want, event, rank, col, chosen_v, want_out, asked, asked_s, chosen_s, small_sem,
    fetch_out, fetch_in, unit_out, unit_in, coef_out, coef_in,
    part, flat, normed, preact, proj, gated, staged, landed,
    out_rows, tall, mat, cosine, expo, grad, cot, gated_cot, pre_cot,
    parts, land_c, stage_x, land_x, stage_z, land_z, hot, side,
    ids_sem, hist_sem, fetch_sem, unit_sem, coef_sem, gat_sem, sca_sem, cot_sem,
    c_sem, x_sem, z_sem,
):
    ix, iz, ic, im = (lax.axis_index(a) for a in ALL)
    nx, nz, nc, nm = NX, NZ, NC, NM
    n = nx * nz * nc * nm
    here_dp = (ix * nz + iz) * nc + ic
    n_dp = nx * nz * nc
    chips = nx * nz * nm
    chip = (ix * nz + iz) * nm + im
    me = ic * chips + chip
    cores = (ic, 1 - ic)
    bases = [pl.multiple_of(core * chips, chips) for core in cores]

    def dp_at(d):
        return (lax.div(d, nz * nc), lax.rem(lax.div(d, nc), nz), lax.rem(d, nc))

    def device(core, q):
        return (lax.div(q, nz * nm), lax.rem(lax.div(q, nm), nz), core, lax.rem(q, nm))

    def chip_at(k):
        return lax.rem(chip + k, chips)

    loads = [
        pltpu.make_async_copy(a, b, load_sem.at[i])
        for i, (a, b) in enumerate(
            [(history_hbm, hist), (cat_hbm, cat), (w_in_hbm, w_in), (w_out_hbm, w_out)]
        )
    ]
    for load in loads:
        load.start()

    barrier = pltpu.get_barrier_semaphore()

    def greet(core, k):
        pl.semaphore_signal(
            barrier, inc=1, device_id=device(core, chip_at(k)), device_id_type=MESH
        )

    def to_both(act):
        act(cores[1], 0)
        for core in cores:
            act(core, 1)

        def one(k, carry):
            for core in cores:
                act(core, k)
            return carry

        lax.fori_loop(2, chips, one, 0, unroll=6)

    to_both(greet)

    slots_kernel(owners_ref, rows_ref, want, event, rank, col)
    want_out[...] = want[...].reshape(want_out.shape)
    chosen_v[...] = event[...].reshape(chosen_v.shape)
    to_smem = pltpu.make_async_copy(chosen_v, chosen_s, small_sem.at[0])
    to_smem.start()
    from_here = lax.div(source_ref[...], SEQ_DEV) == here_dp
    local = jnp.where(from_here, lax.rem(source_ref[...], SEQ_DEV), 0)
    local = jnp.max(local, axis=1, keepdims=True)
    seq_v[...] = jnp.broadcast_to(local, (n_dp, 128)).reshape(seq_v.shape)
    seq_copy = pltpu.make_async_copy(seq_v, seq_s, small_sem.at[1])
    seq_copy.start()
    lengths = [lengths_s[source_s[here_dp * SEQ_DEV + i]] for i in range(SEQ_DEV)]
    for i, length in enumerate(lengths):
        count_ref[i * STEPS : (i + 1) * STEPS, :] = jnp.full((STEPS, 1), length).astype(F32)
    loads[0].wait()
    seq_copy.wait()

    def stage(d, carry):
        hist_out[d] = hist[seq_s[d, 0, 0]]
        return carry

    lax.fori_loop(0, n_dp, stage, 0, unroll=4)
    loads[1].wait()
    chunks, lanes = cat.shape[1] // 128, 128
    for i in range(cat.shape[0] // chips):
        rows = slice(i * chips, (i + 1) * chips)
        for c in range(chunks):
            tall[pl.ds(c, chips, stride=chunks), :] = cat[rows, c * lanes : (c + 1) * lanes].astype(F32)
        tiles[rows] = tall[...].reshape(chips, chunks, lanes).astype(BF16)
    pl.semaphore_wait(barrier, n - 1)

    def push(src, dst, sems, core, q):
        pltpu.make_async_remote_copy(
            src_ref=src.at[core * chips + q],
            dst_ref=dst.at[me],
            send_sem=sems.at[0],
            recv_sem=sems.at[1],
            device_id=device(core, q),
            device_id_type=MESH,
        ).start()

    def finish(ref, sems, which, count):
        block = ref.at[pl.ds(0, count)]
        pltpu.make_async_copy(block, block, sems.at[which]).wait()

    to_both(lambda core, k: push(want_out, asked, ids_sem, core, chip_at(k)))
    asked[me] = want_out[me]

    def send_history(k, carry):
        d = lax.rem(here_dp + k, n_dp)
        pltpu.make_async_remote_copy(
            src_ref=hist_out.at[d],
            dst_ref=arrived.at[here_dp],
            send_sem=hist_sem.at[0],
            recv_sem=hist_sem.at[1],
            device_id=dp_at(d) + (im,),
            device_id_type=MESH,
        ).start()
        return carry

    lax.fori_loop(1, n_dp, send_history, 0)
    arrived[here_dp] = hist_out[here_dp]

    to_smem.wait()
    finish(asked, ids_sem, 1, n - 1)
    to_smem = pltpu.make_async_copy(asked, asked_s, small_sem.at[1])
    to_smem.start()
    to_smem.wait()

    def fill(out, d, table, idx):
        for r in range(CAP):
            out[d, r] = table[jnp.maximum(idx[d, 0, r], 0)]

    def serve(out, into, table, idx, sems, core, first, last, unroll):
        fill(out, core * chips + chip_at(first), table, idx)

        def one(k, carry):
            fill(out, core * chips + chip_at(k), table, idx)
            push(out, into, sems, core, chip_at(k - 1))
            return carry

        lax.fori_loop(first + 1, last, one, 0, unroll=unroll)
        push(out, into, sems, core, chip_at(last - 1))

    def serve_rows(part, first, last, unroll):
        serve(fetch_out, fetch_in, tiles, asked_s, fetch_sem.at[part], cores[part], first, last, unroll)

    serve_rows(0, 1, chips, 6)
    fill(fetch_out, me, tiles, asked_s)
    fetch_in[me] = fetch_out[me]

    peers = [lax.rem(im + k, nm) for k in range(1, nm)]
    finish(arrived, hist_sem, 1, n_dp - 1)
    for s in range(SEQ_DEV):
        part[s * STEPS : (s + 1) * STEPS, :] = arrived[lax.div(source_s[here_dp * SEQ_DEV + s], SEQ_DEV)]
    rows_all, cols_here = part.shape
    width = flat.shape[1]
    quarter = rows_all // nm
    mine = pl.ds(pl.multiple_of(im * cols_here, cols_here), cols_here)
    gathers = [
        pltpu.make_async_remote_copy(
            src_ref=part,
            dst_ref=flat.at[:, mine],
            send_sem=gat_sem.at[0, i],
            recv_sem=gat_sem.at[1, i],
            device_id=(ix, iz, ic, p),
            device_id_type=MESH,
        )
        for i, p in enumerate(peers)
    ]
    for copy in gathers:
        copy.start()
    serve_rows(1, 0, chips // 2, 7)
    flat[:, mine] = part[...]
    for copy in gathers:
        copy.wait()

    loads[2].wait()
    loads[3].wait()
    for b in range(nm):
        rows = slice(b * quarter, (b + 1) * quarter)
        scaled, _ = center(flat[rows, :].astype(F32))
        normed[rows, :] = scaled.astype(BF16)
    heads = cols_here // DH
    for c in range(4):
        z = jnp.dot(normed[...], w_in[c], preferred_element_type=F32)
        preact[c] = z
        proj[c] = (z * sigmoid(z)).astype(BF16)

    def forward(rows, cols):
        count = count_ref[rows, :]
        scores, mask = attention_weights(proj[2, rows, cols], proj[3, rows, cols], count)
        weights = jnp.where(mask, scores * sigmoid(scores) / count, 0.0).astype(BF16)
        mixed = jnp.dot(weights, proj[1, rows, cols], preferred_element_type=F32)
        scaled, inv = center(mixed)
        return scores, mask, weights, scaled, inv

    for b in range(nm):
        for h in range(heads):
            rows = slice(b * quarter, (b + 1) * quarter)
            cols = slice(h * DH, (h + 1) * DH)
            scaled = forward(rows, cols)[3]
            gated[rows, cols] = (scaled * proj[0, rows, cols].astype(F32)).astype(BF16)

    def block(m):
        rows = pl.ds(pl.multiple_of(m * quarter, quarter), quarter)
        return jnp.dot(gated[rows, :], w_out[...], preferred_element_type=F32)

    for i, p in enumerate(peers):
        staged[i] = block(p).astype(BF16)
    copies = [
        pltpu.make_async_remote_copy(
            src_ref=staged.at[i],
            dst_ref=landed.at[i],
            send_sem=sca_sem.at[0, i],
            recv_sem=sca_sem.at[1, i],
            device_id=(ix, iz, ic, p),
            device_id_type=MESH,
        )
        for i, p in enumerate(peers)
    ]
    for copy in copies:
        copy.start()
    serve_rows(1, chips // 2, chips, 7)
    own = pl.ds(pl.multiple_of(im * quarter, quarter), quarter)
    total = block(im) + flat[own, :].astype(F32)
    for i, copy in enumerate(copies):
        copy.wait()
        total = total + landed[i].astype(F32)
    out_rows[...] = total
    inv_out = 1.0 / jnp.sqrt(jnp.sum(total * total, axis=-1, keepdims=True) + epsilon_unit)
    unit = total * inv_out
    unit_b = unit.astype(BF16)

    for c in range(chunks):
        tall[pl.ds(c, quarter, stride=chunks), :] = unit[:, c * lanes : (c + 1) * lanes]
    unit_tiles = tiles.at[pl.ds(0, quarter)]
    unit_tiles[...] = tall[...].reshape(quarter, chunks, lanes).astype(BF16)

    def serve_units(part, first, last, unroll):
        serve(unit_out, unit_in, unit_tiles, chosen_s, unit_sem.at[part], cores[part], first, last, unroll)

    serve_units(0, 1, chips, 6)
    fill(unit_out, me, unit_tiles, chosen_s)
    unit_in[me] = unit_out[me]

    def spread(ref, base, r):
        tall[...] = ref[pl.ds(base, chips), r].astype(F32).reshape(chips * chunks, lanes)

    sums = jnp.zeros((1, quarter), F32)
    inverse = {}
    for p, base in enumerate(bases):
        finish(fetch_in, fetch_sem.at[p], 1, chips - 1 + p)
        ranks = rank[pl.ds(base, chips), :]
        for r in range(CAP):
            i = p * CAP + r
            spread(fetch_in, base, r)
            squares = jnp.zeros((chips, lanes), F32)
            for c in range(chunks):
                chunk = tall[pl.ds(c, chips, stride=chunks), :]
                squares = squares + chunk * chunk
                mat[i * chips : (i + 1) * chips, c * lanes : (c + 1) * lanes] = chunk.astype(BF16)
            inv = 1.0 / jnp.sqrt(jnp.sum(squares, axis=-1, keepdims=True) + epsilon_unit)
            inverse[i] = inv
            dots = lax.dot_general(
                mat[i * chips : (i + 1) * chips, :], unit_b, OVER_COLS, preferred_element_type=F32
            )
            cos = dots * inv
            ex = jnp.where(ranks == r, jnp.exp(cos / cosine_divisor), 0.0)
            cosine[i] = cos
            expo[i] = ex
            sums = sums + jnp.sum(ex, axis=0, keepdims=True)
    lane_q = lax.broadcasted_iota(jnp.int32, (1, quarter), 1)
    valid = jnp.zeros((1, quarter), F32)
    for i in range(quarter // STEPS):
        length = lengths_s[source_s[here_dp * SEQ_DEV + im * (quarter // STEPS) + i]]
        inside = (lane_q >= i * STEPS) & (lane_q < (i + 1) * STEPS) & (lane_q - i * STEPS < length)
        valid = jnp.where(inside, 1.0, valid)
    scale = valid / sums
    lane = lax.broadcasted_iota(jnp.int32, (chips, lanes), 1)
    slope = jnp.zeros((quarter, width), F32)
    for p, base in enumerate(bases):
        ranks = rank[pl.ds(base, chips), :]
        first = (col[pl.ds(base, chips), :] == 0).astype(F32) * valid
        coef = jnp.zeros((chips, lanes), F32)
        for r in range(CAP):
            i = p * CAP + r
            share = expo[i] * scale - jnp.where(ranks == r, first, 0.0)
            weight = share * (inverse[i] / cosine_divisor)
            slope = slope + lax.dot_general(
                weight.astype(BF16), mat[i * chips : (i + 1) * chips, :], OVER_ROWS,
                preferred_element_type=F32,
            )
            a = jnp.sum(weight, axis=-1, keepdims=True)
            b = jnp.sum(weight * cosine[i], axis=-1, keepdims=True) * inverse[i]
            coef = jnp.where(lane == r, a, coef)
            coef = jnp.where(lane == r + 8, b, coef)
        coef_out[pl.ds(base, chips)] = coef.reshape(chips, 1, lanes)
    along = jnp.sum(unit * slope, axis=-1, keepdims=True)
    grad[...] = ((slope - unit * along) * inv_out).astype(BF16)
    copies = [
        pltpu.make_async_remote_copy(
            src_ref=grad,
            dst_ref=cot.at[own, :],
            send_sem=cot_sem.at[0, i],
            recv_sem=cot_sem.at[1, i],
            device_id=(ix, iz, ic, p),
            device_id_type=MESH,
        )
        for i, p in enumerate(peers)
    ]
    for copy in copies:
        copy.start()
    to_both(lambda core, k: push(coef_out, coef_in, coef_sem, core, chip_at(k)))
    serve_units(1, 0, chips, 1)
    coef_in[me] = coef_out[me]
    cot[own, :] = grad[...]
    for copy in copies:
        copy.wait()

    gated_cot[...] = lax.dot_general(
        cot[...], w_out[...], OVER_COLS, preferred_element_type=F32
    ).astype(BF16)
    for b in range(nm):
        for h in range(heads):
            rows = slice(b * quarter, (b + 1) * quarter)
            cols = slice(h * DH, (h + 1) * DH)
            count = count_ref[rows, :]
            scores, mask, weights, scaled, inv = forward(rows, cols)
            gc = gated_cot[rows, cols].astype(F32)
            d_gating = gc * scaled
            d_scaled = gc * proj[0, rows, cols].astype(F32)
            d_mixed = inv * (
                d_scaled
                - jnp.mean(d_scaled, axis=-1, keepdims=True)
                - scaled * jnp.mean(d_scaled * scaled, axis=-1, keepdims=True)
            )
            d_mixed = d_mixed.astype(BF16)
            d_weights = lax.dot_general(
                d_mixed, proj[1, rows, cols], OVER_COLS, preferred_element_type=F32
            )
            d_weights = d_weights.astype(BF16).astype(F32)
            d_values = lax.dot_general(weights, d_mixed, OVER_ROWS, preferred_element_type=F32)
            d_scores = jnp.where(
                mask, d_weights * silu_slope(scores) * (DH**-0.5) / count, 0.0
            ).astype(BF16)
            d_queries = jnp.dot(d_scores, proj[3, rows, cols], preferred_element_type=F32)
            d_keys = lax.dot_general(
                d_scores, proj[2, rows, cols], OVER_ROWS, preferred_element_type=F32
            )
            for c, d in enumerate((d_gating, d_values, d_queries, d_keys)):
                at = slice(c * cols_here + h * DH, c * cols_here + (h + 1) * DH)
                pre_cot[rows, at] = (
                    d.astype(BF16).astype(F32) * silu_slope(preact[c, rows, cols])
                ).astype(BF16)

    block_rows = width // nx
    groups = parts.shape[0]
    peer_c = (ix, iz, 1 - ic, im)
    swaps = []
    order = [lax.rem(ix + k, nx) for k in list(range(1, nx)) + [0]]
    for i, p in enumerate(order):
        at = pl.ds(pl.multiple_of(p * block_rows, block_rows), block_rows)
        res = lax.dot_general(normed[:, at], pre_cot[...], OVER_ROWS, preferred_element_type=F32)
        for c in range(4):
            parts[c, p] = (
                res[:, c * cols_here : (c + 1) * cols_here].astype(BF16).reshape(parts.shape[2:])
            )
        res = lax.dot_general(cot[:, at], gated[...], OVER_ROWS, preferred_element_type=F32)
        parts[4, p] = res.astype(BF16).reshape(parts.shape[2:])
        swaps.append(
            pltpu.make_async_remote_copy(
                src_ref=parts.at[:, p, :, 1 - ic],
                dst_ref=land_c.at[:, p],
                send_sem=c_sem.at[0, i],
                recv_sem=c_sem.at[1, i],
                device_id=peer_c,
                device_id_type=MESH,
            )
        )
        swaps[-1].start()
    copies = []
    for i in range(nx - 1):
        p = order[i]
        swaps[i].wait()
        stage_x[i] = (parts[:, p, :, ic].astype(F32) + land_c[:, p].astype(F32)).astype(BF16)
        copies.append(
            pltpu.make_async_remote_copy(
                src_ref=stage_x.at[i],
                dst_ref=land_x.at[i],
                send_sem=x_sem.at[0, i],
                recv_sem=x_sem.at[1, i],
                device_id=(p, iz, ic, im),
                device_id_type=MESH,
            )
        )
        copies[-1].start()
    swaps[nx - 1].wait()
    held = parts[:, ix, :, ic].astype(F32) + land_c[:, ix].astype(F32)
    for i, copy in enumerate(copies):
        copy.wait()
        held = held + land_x[i].astype(F32)
    stage_z[...] = held.astype(BF16)
    copies = []
    for i in range(nz - 1):
        p = lax.rem(iz + 1 + i, nz)
        copies.append(
            pltpu.make_async_remote_copy(
                src_ref=stage_z.at[:, p],
                dst_ref=land_z.at[i],
                send_sem=z_sem.at[0, i],
                recv_sem=z_sem.at[1, i],
                device_id=(ix, p, ic, im),
                device_id_type=MESH,
            )
        )
        copies[-1].start()

    finish(coef_in, coef_sem, 1, n - 1)
    rows_cat = cat.shape[0]
    row = lax.broadcasted_iota(jnp.int32, (chips, rows_cat), 1)

    def catalogue_half(p):
        base = bases[p]
        finish(unit_in, unit_sem.at[p], 1, chips - 1 + p)
        wanted = asked[pl.ds(base, chips)].reshape(chips, lanes)
        coef = coef_in[pl.ds(base, chips)].reshape(chips, lanes)
        half = slice(p * CAP * chips, (p + 1) * CAP * chips)
        for r in range(CAP):
            spread(unit_in, base, r)
            a = coef[:, r : r + 1]
            b = coef[:, r + 8 : r + 9]
            high = b.astype(BF16).astype(F32)
            span = slice((p * CAP + r) * chips, (p * CAP + r + 1) * chips)
            for c in range(chunks):
                chunk = tall[pl.ds(c, chips, stride=chunks), :]
                mat[span, c * lanes : (c + 1) * lanes] = (chunk * a).astype(BF16)
            side[span, :] = jnp.where(
                lane == 0, high, jnp.where(lane == 1, b - high, 0.0)
            ).astype(BF16)
            hot[span, :] = (wanted[:, r : r + 1] == row).astype(F32).astype(BF16)
        both = lax.dot_general(hot[half, :], side[half, :], OVER_ROWS, preferred_element_type=F32)
        b_row = both[:, 0:1] + both[:, 1:2]
        for c in range(0, width, 256):
            at = slice(c, c + 256)
            res = lax.dot_general(hot[half, :], mat[half, at], OVER_ROWS, preferred_element_type=F32)
            res = res - b_row * cat[:, at].astype(F32)
            cat_grad_ref[:, at] = res if p == 0 else cat_grad_ref[:, at] + res

    catalogue_half(0)
    held = stage_z[:, iz].astype(F32)
    for i, copy in enumerate(copies):
        copy.wait()
        held = held + land_z[i].astype(F32)
    sums_ref[...] = held
    catalogue_half(1)

    finish(want_out, ids_sem, 0, n - 1)
    finish(hist_out, hist_sem, 0, n_dp - 1)
    for p in range(nc):
        finish(fetch_out, fetch_sem.at[p], 0, chips - 1 + p)
        finish(unit_out, unit_sem.at[p], 0, chips - 1 + p)
    finish(coef_out, coef_sem, 0, n - 1)


ALL = ("x", "z", "c", "mp")
DP = ("x", "z", "c")
NX, NZ, NC, NM = 4, 8, 2, 4
SEQ_DEV = 16


def step(source, lengths, source_2d, owners_t, rows_t, history, catalogue, w_in, w_out):
    n_dp = NX * NZ * NC
    n = n_dp * NM
    seqs, steps, cols = history.shape
    rows_all = seqs * steps
    rows_cat, width = catalogue.shape
    quarter = rows_all // NM
    chunks = width // 128
    rows_out = width // n_dp
    dma = pltpu.SemaphoreType.DMA
    V = pltpu.VMEM
    I32 = jnp.int32
    anyw = pl.BlockSpec(memory_space=pl.ANY)
    message = (n, CAP, chunks, 128)
    scratch = [
        V((rows_all, 1), F32), V((n_dp, 1, 128), I32), pltpu.SMEM((n_dp, 1, 128), I32),
        V(history.shape, BF16), V((n_dp, steps, cols), BF16), V((n_dp, steps, cols), BF16),
        V((rows_cat, chunks, 128), BF16), V(catalogue.shape, BF16), V(w_in.shape, BF16), V(w_out.shape, BF16), dma((4,)),
        V((n, 128), I32), V((n, 128), I32), V((n, quarter), I32), V((n, quarter), I32),
        V((n, 1, 128), I32), V((n, 1, 128), I32), V((n, 1, 128), I32),
        pltpu.SMEM((n, 1, 128), I32), pltpu.SMEM((n, 1, 128), I32), dma((2,)),
        V(message, BF16), V(message, BF16), V(message, BF16), V(message, BF16),
        V((n, 1, 128), F32), V((n, 1, 128), F32),
        V((rows_all, cols), BF16), V((rows_all, width), BF16), V((rows_all, width), BF16),
        V((4, rows_all, cols), F32), V((4, rows_all, cols), BF16), V((rows_all, cols), BF16),
        V((NM - 1, quarter, width), BF16), V((NM - 1, quarter, width), BF16),
        V((quarter, width), F32), V((n // NC * chunks, 128), F32), V((CAP * n, width), BF16),
        V((NC * CAP, n // NC, quarter), F32), V((NC * CAP, n // NC, quarter), F32), V((quarter, width), BF16),
        V((rows_all, width), BF16), V((rows_all, cols), BF16), V((rows_all, 4 * cols), BF16),
        V((5, NX, NZ, NC, rows_out, cols), BF16), V((5, NX, NZ, rows_out, cols), BF16),
        V((NX - 1, 5, NZ, rows_out, cols), BF16), V((NX - 1, 5, NZ, rows_out, cols), BF16),
        V((5, NZ, rows_out, cols), BF16), V((NZ - 1, 5, rows_out, cols), BF16),
        V((CAP * n, rows_cat), BF16), V((CAP * n, 128), BF16),
        dma((2,)), dma((2,)), dma((NC, 2)), dma((NC, 2)), dma((2,)),
        dma((2, NM - 1)), dma((2, NM - 1)), dma((2, NM - 1)),
        dma((2, NX)), dma((2, NX - 1)), dma((2, NZ - 1)),
    ]
    return pl.pallas_call(
        step_kernel,
        out_shape=(sds((rows_cat, width), F32), sds((5, rows_out, cols), F32)),
        in_specs=[SM, SM, VM, VM, VM] + [anyw] * 4,
        out_specs=(VM, VM),
        scratch_shapes=scratch,
        compiler_params=params(collective_id=0, has_side_effects=True),
        name="step",
    )(source, lengths, source_2d, owners_t, rows_t, history, catalogue, w_in, w_out)


def per_device(history, lengths, source, owners, item_rows, catalogue, w_in, w_out):
    cat_grad, sums = step(
        source,
        lengths,
        source.reshape(NX * NZ * NC, SEQ_DEV),
        owners.T,
        item_rows.T,
        history,
        catalogue,
        w_in,
        w_out,
    )
    return (sums[:4], sums[4].T, cat_grad)


def solution(mesh):
    split = Mesh(mesh.devices.reshape(NX, NZ, NC, NM), ALL)
    placed = (
        P(DP, None, "mp"),
        P(),
        P(),
        P(ALL, None),
        P(ALL, None),
        P(ALL, None),
        P(None, None, "mp"),
        P("mp", None),
    )
    return jax.shard_map(
        per_device,
        mesh=split,
        in_specs=placed,
        out_specs=(P(None, DP, "mp"), P("mp", DP), P(ALL, None)),
        check_vma=False,
    )
```

```python
import functools

import jax
import jax.numpy as jnp
from jax import lax
from jax.experimental import pallas as pl
from jax.experimental.pallas import tpu as pltpu
from jax.sharding import Mesh, PartitionSpec as P

DH = 128
CAP = 6
MESH = pl.DeviceIdType.MESH
F32 = jnp.float32
BF16 = jnp.bfloat16

cosine_divisor = 0.05
epsilon_norm = 1e-05
epsilon_unit = 1e-06

VM = pl.BlockSpec(memory_space=pltpu.VMEM)
SM = pl.BlockSpec(memory_space=pltpu.SMEM)


def sds(shape, dtype):
    return jax.ShapeDtypeStruct(shape, dtype)


def params(**kw):
    return pltpu.CompilerParams(vmem_limit_bytes=60 * 1024 * 1024, **kw)


def slots_kernel(own_ref, row_ref, want_ref, event_ref, rank_ref, col_ref):
    owners_n, events = rank_ref.shape
    who = lax.broadcasted_iota(jnp.int32, (owners_n, events), 0)
    named = jnp.zeros((owners_n, events), F32)
    rows = jnp.zeros((owners_n, events), jnp.int32)
    cols = jnp.zeros((owners_n, events), jnp.int32)
    own = own_ref[...]
    core = lax.rem(lax.div(own, NM), NC)
    own = core * (owners_n // NC) + lax.div(own, NM * NC) * NM + lax.rem(own, NM)
    for j in range(own_ref.shape[0]):
        mask = own[j : j + 1, :] == who
        named = jnp.where(mask, 1.0, named)
        rows = jnp.where(mask, row_ref[j : j + 1, :], rows)
        cols = jnp.where(mask, j, cols)
    before = (
        lax.broadcasted_iota(jnp.int32, (events, events), 0)
        < lax.broadcasted_iota(jnp.int32, (events, events), 1)
    ).astype(F32)
    rank = jnp.dot(
        named.astype(BF16), before.astype(BF16), preferred_element_type=F32
    ).astype(jnp.int32)
    rank = jnp.where(named > 0.0, rank, -1)
    rank_ref[...] = rank
    col_ref[...] = cols
    event = lax.broadcasted_iota(jnp.int32, (owners_n, events), 1)
    lane = lax.broadcasted_iota(jnp.int32, want_ref.shape, 1)
    want = jnp.full(want_ref.shape, -1, jnp.int32)
    chosen = jnp.zeros(want_ref.shape, jnp.int32)
    for r in range(CAP):
        here = rank == r
        row_r = jnp.max(jnp.where(here, rows, -1), axis=1, keepdims=True)
        event_r = jnp.max(jnp.where(here, event, 0), axis=1, keepdims=True)
        want = jnp.where(lane == r, row_r, want)
        chosen = jnp.where(lane == r, event_r, chosen)
    want_ref[...] = want
    event_ref[...] = chosen


OVER_ROWS = (((0,), (0,)), ((), ()))
OVER_COLS = (((1,), (1,)), ((), ()))


def sigmoid(v):
    return 1.0 / (1.0 + jnp.exp(-v))


def silu_slope(v):
    s = sigmoid(v)
    return s * (1.0 + v * (1.0 - s))


def center(v):
    moved = v - jnp.mean(v, axis=-1, keepdims=True)
    inv = 1.0 / jnp.sqrt(jnp.mean(moved * moved, axis=-1, keepdims=True) + epsilon_norm)
    return moved * inv, inv


def attention_weights(q, k, count):
    n = q.shape[0]
    scores = lax.dot_general(q, k, OVER_COLS, preferred_element_type=F32) * (DH**-0.5)
    t = lax.broadcasted_iota(jnp.int32, (n, n), 0)
    s = lax.broadcasted_iota(jnp.int32, (n, n), 1)
    first = t - lax.rem(t, STEPS)
    mask = (s >= first) & (s <= t) & ((s - first).astype(F32) < count)
    return scores, mask


STEPS = 32


def step_kernel(
    source_s, lengths_s, source_ref, owners_ref, rows_ref,
    history_hbm, cat_hbm, w_in_hbm, w_out_hbm,
    cat_grad_ref, sums_ref,
    count_ref, seq_v, seq_s, hist, hist_out, arrived, tiles, cat, w_in, w_out, load_sem,
    want, event, rank, col, chosen_v, want_out, asked, asked_s, chosen_s, small_sem,
    fetch_out, fetch_in, unit_out, unit_in, coef_out, coef_in,
    part, flat, normed, preact, proj, gated, staged, landed,
    out_rows, tall, mat, cosine, expo, grad, cot, gated_cot, pre_cot,
    parts, land_c, stage_x, land_x, stage_z, land_z, hot, side,
    ids_sem, hist_sem, fetch_sem, unit_sem, coef_sem, gat_sem, sca_sem, cot_sem,
    c_sem, x_sem, z_sem,
):
    ix, iz, ic, im = (lax.axis_index(a) for a in ALL)
    nx, nz, nc, nm = NX, NZ, NC, NM
    n = nx * nz * nc * nm
    here_dp = (ix * nz + iz) * nc + ic
    n_dp = nx * nz * nc
    chips = nx * nz * nm
    chip = (ix * nz + iz) * nm + im
    me = ic * chips + chip
    cores = (ic, 1 - ic)
    bases = [pl.multiple_of(core * chips, chips) for core in cores]

    def dp_at(d):
        return (lax.div(d, nz * nc), lax.rem(lax.div(d, nc), nz), lax.rem(d, nc))

    def device(core, q):
        return (lax.div(q, nz * nm), lax.rem(lax.div(q, nm), nz), core, lax.rem(q, nm))

    def chip_at(k):
        return lax.rem(chip + k, chips)

    loads = [
        pltpu.make_async_copy(a, b, load_sem.at[i])
        for i, (a, b) in enumerate(
            [(history_hbm, hist), (cat_hbm, cat), (w_in_hbm, w_in), (w_out_hbm, w_out)]
        )
    ]
    for load in loads:
        load.start()

    barrier = pltpu.get_barrier_semaphore()

    def greet(core, k):
        pl.semaphore_signal(
            barrier, inc=1, device_id=device(core, chip_at(k)), device_id_type=MESH
        )

    def to_both(act):
        act(cores[1], 0)
        for core in cores:
            act(core, 1)

        def one(k, carry):
            for core in cores:
                act(core, k)
            return carry

        lax.fori_loop(2, chips, one, 0, unroll=6)

    to_both(greet)

    slots_kernel(owners_ref, rows_ref, want, event, rank, col)
    want_out[...] = want[...].reshape(want_out.shape)
    chosen_v[...] = event[...].reshape(chosen_v.shape)
    to_smem = pltpu.make_async_copy(chosen_v, chosen_s, small_sem.at[0])
    to_smem.start()
    from_here = lax.div(source_ref[...], SEQ_DEV) == here_dp
    local = jnp.where(from_here, lax.rem(source_ref[...], SEQ_DEV), 0)
    local = jnp.max(local, axis=1, keepdims=True)
    seq_v[...] = jnp.broadcast_to(local, (n_dp, 128)).reshape(seq_v.shape)
    seq_copy = pltpu.make_async_copy(seq_v, seq_s, small_sem.at[1])
    seq_copy.start()
    lengths = [lengths_s[source_s[here_dp * SEQ_DEV + i]] for i in range(SEQ_DEV)]
    for i, length in enumerate(lengths):
        count_ref[i * STEPS : (i + 1) * STEPS, :] = jnp.full((STEPS, 1), length).astype(F32)
    loads[0].wait()
    seq_copy.wait()

    def stage(d, carry):
        hist_out[d] = hist[seq_s[d, 0, 0]]
        return carry

    lax.fori_loop(0, n_dp, stage, 0, unroll=4)
    loads[1].wait()
    chunks, lanes = cat.shape[1] // 128, 128
    for i in range(cat.shape[0] // chips):
        rows = slice(i * chips, (i + 1) * chips)
        for c in range(chunks):
            tall[pl.ds(c, chips, stride=chunks), :] = cat[rows, c * lanes : (c + 1) * lanes].astype(F32)
        tiles[rows] = tall[...].reshape(chips, chunks, lanes).astype(BF16)
    pl.semaphore_wait(barrier, n - 1)

    def push(src, dst, sems, core, q):
        pltpu.make_async_remote_copy(
            src_ref=src.at[core * chips + q],
            dst_ref=dst.at[me],
            send_sem=sems.at[0],
            recv_sem=sems.at[1],
            device_id=device(core, q),
            device_id_type=MESH,
        ).start()

    def finish(ref, sems, which, count):
        block = ref.at[pl.ds(0, count)]
        pltpu.make_async_copy(block, block, sems.at[which]).wait()

    to_both(lambda core, k: push(want_out, asked, ids_sem, core, chip_at(k)))
    asked[me] = want_out[me]

    def send_history(k, carry):
        d = lax.rem(here_dp + k, n_dp)
        pltpu.make_async_remote_copy(
            src_ref=hist_out.at[d],
            dst_ref=arrived.at[here_dp],
            send_sem=hist_sem.at[0],
            recv_sem=hist_sem.at[1],
            device_id=dp_at(d) + (im,),
            device_id_type=MESH,
        ).start()
        return carry

    lax.fori_loop(1, n_dp, send_history, 0)
    arrived[here_dp] = hist_out[here_dp]

    to_smem.wait()
    finish(asked, ids_sem, 1, n - 1)
    to_smem = pltpu.make_async_copy(asked, asked_s, small_sem.at[1])
    to_smem.start()
    to_smem.wait()

    def fill(out, d, table, idx):
        for r in range(CAP):
            out[d, r] = table[jnp.maximum(idx[d, 0, r], 0)]

    def serve(out, into, table, idx, sems, core, first, last, unroll):
        fill(out, core * chips + chip_at(first), table, idx)

        def one(k, carry):
            fill(out, core * chips + chip_at(k), table, idx)
            push(out, into, sems, core, chip_at(k - 1))
            return carry

        lax.fori_loop(first + 1, last, one, 0, unroll=unroll)
        push(out, into, sems, core, chip_at(last - 1))

    def serve_rows(part, first, last, unroll):
        serve(fetch_out, fetch_in, tiles, asked_s, fetch_sem.at[part], cores[part], first, last, unroll)

    serve_rows(0, 1, chips, 6)
    fill(fetch_out, me, tiles, asked_s)
    fetch_in[me] = fetch_out[me]

    peers = [lax.rem(im + k, nm) for k in range(1, nm)]
    finish(arrived, hist_sem, 1, n_dp - 1)
    for s in range(SEQ_DEV):
        part[s * STEPS : (s + 1) * STEPS, :] = arrived[lax.div(source_s[here_dp * SEQ_DEV + s], SEQ_DEV)]
    rows_all, cols_here = part.shape
    width = flat.shape[1]
    quarter = rows_all // nm
    mine = pl.ds(pl.multiple_of(im * cols_here, cols_here), cols_here)
    gathers = [
        pltpu.make_async_remote_copy(
            src_ref=part,
            dst_ref=flat.at[:, mine],
            send_sem=gat_sem.at[0, i],
            recv_sem=gat_sem.at[1, i],
            device_id=(ix, iz, ic, p),
            device_id_type=MESH,
        )
        for i, p in enumerate(peers)
    ]
    for copy in gathers:
        copy.start()
    serve_rows(1, 0, chips // 2, 7)
    flat[:, mine] = part[...]
    for copy in gathers:
        copy.wait()

    loads[2].wait()
    loads[3].wait()
    for b in range(nm):
        rows = slice(b * quarter, (b + 1) * quarter)
        scaled, _ = center(flat[rows, :].astype(F32))
        normed[rows, :] = scaled.astype(BF16)
    heads = cols_here // DH
    for c in range(4):
        z = jnp.dot(normed[...], w_in[c], preferred_element_type=F32)
        preact[c] = z
        proj[c] = (z * sigmoid(z)).astype(BF16)

    def forward(rows, cols):
        count = count_ref[rows, :]
        scores, mask = attention_weights(proj[2, rows, cols], proj[3, rows, cols], count)
        weights = jnp.where(mask, scores * sigmoid(scores) / count, 0.0).astype(BF16)
        mixed = jnp.dot(weights, proj[1, rows, cols], preferred_element_type=F32)
        scaled, inv = center(mixed)
        return scores, mask, weights, scaled, inv

    for b in range(nm):
        for h in range(heads):
            rows = slice(b * quarter, (b + 1) * quarter)
            cols = slice(h * DH, (h + 1) * DH)
            scaled = forward(rows, cols)[3]
            gated[rows, cols] = (scaled * proj[0, rows, cols].astype(F32)).astype(BF16)

    def block(m):
        rows = pl.ds(pl.multiple_of(m * quarter, quarter), quarter)
        return jnp.dot(gated[rows, :], w_out[...], preferred_element_type=F32)

    for i, p in enumerate(peers):
        staged[i] = block(p).astype(BF16)
    copies = [
        pltpu.make_async_remote_copy(
            src_ref=staged.at[i],
            dst_ref=landed.at[i],
            send_sem=sca_sem.at[0, i],
            recv_sem=sca_sem.at[1, i],
            device_id=(ix, iz, ic, p),
            device_id_type=MESH,
        )
        for i, p in enumerate(peers)
    ]
    for copy in copies:
        copy.start()
    serve_rows(1, chips // 2, chips, 7)
    own = pl.ds(pl.multiple_of(im * quarter, quarter), quarter)
    total = block(im) + flat[own, :].astype(F32)
    for i, copy in enumerate(copies):
        copy.wait()
        total = total + landed[i].astype(F32)
    out_rows[...] = total
    inv_out = 1.0 / jnp.sqrt(jnp.sum(total * total, axis=-1, keepdims=True) + epsilon_unit)
    unit = total * inv_out
    unit_b = unit.astype(BF16)

    for c in range(chunks):
        tall[pl.ds(c, quarter, stride=chunks), :] = unit[:, c * lanes : (c + 1) * lanes]
    unit_tiles = tiles.at[pl.ds(0, quarter)]
    unit_tiles[...] = tall[...].reshape(quarter, chunks, lanes).astype(BF16)

    def serve_units(part, first, last, unroll):
        serve(unit_out, unit_in, unit_tiles, chosen_s, unit_sem.at[part], cores[part], first, last, unroll)

    serve_units(0, 1, chips, 6)
    fill(unit_out, me, unit_tiles, chosen_s)
    unit_in[me] = unit_out[me]

    def spread(ref, base, r):
        tall[...] = ref[pl.ds(base, chips), r].astype(F32).reshape(chips * chunks, lanes)

    sums = jnp.zeros((1, quarter), F32)
    inverse = {}
    for p, base in enumerate(bases):
        finish(fetch_in, fetch_sem.at[p], 1, chips - 1 + p)
        ranks = rank[pl.ds(base, chips), :]
        for r in range(CAP):
            i = p * CAP + r
            spread(fetch_in, base, r)
            squares = jnp.zeros((chips, lanes), F32)
            for c in range(chunks):
                chunk = tall[pl.ds(c, chips, stride=chunks), :]
                squares = squares + chunk * chunk
                mat[i * chips : (i + 1) * chips, c * lanes : (c + 1) * lanes] = chunk.astype(BF16)
            inv = 1.0 / jnp.sqrt(jnp.sum(squares, axis=-1, keepdims=True) + epsilon_unit)
            inverse[i] = inv
            dots = lax.dot_general(
                mat[i * chips : (i + 1) * chips, :], unit_b, OVER_COLS, preferred_element_type=F32
            )
            cos = dots * inv
            ex = jnp.where(ranks == r, jnp.exp(cos / cosine_divisor), 0.0)
            cosine[i] = cos
            expo[i] = ex
            sums = sums + jnp.sum(ex, axis=0, keepdims=True)
    lane_q = lax.broadcasted_iota(jnp.int32, (1, quarter), 1)
    valid = jnp.zeros((1, quarter), F32)
    for i in range(quarter // STEPS):
        length = lengths_s[source_s[here_dp * SEQ_DEV + im * (quarter // STEPS) + i]]
        inside = (lane_q >= i * STEPS) & (lane_q < (i + 1) * STEPS) & (lane_q - i * STEPS < length)
        valid = jnp.where(inside, 1.0, valid)
    scale = valid / sums
    lane = lax.broadcasted_iota(jnp.int32, (chips, lanes), 1)
    slope = jnp.zeros((quarter, width), F32)
    for p, base in enumerate(bases):
        ranks = rank[pl.ds(base, chips), :]
        first = (col[pl.ds(base, chips), :] == 0).astype(F32) * valid
        coef = jnp.zeros((chips, lanes), F32)
        for r in range(CAP):
            i = p * CAP + r
            share = expo[i] * scale - jnp.where(ranks == r, first, 0.0)
            weight = share * (inverse[i] / cosine_divisor)
            slope = slope + lax.dot_general(
                weight.astype(BF16), mat[i * chips : (i + 1) * chips, :], OVER_ROWS,
                preferred_element_type=F32,
            )
            a = jnp.sum(weight, axis=-1, keepdims=True)
            b = jnp.sum(weight * cosine[i], axis=-1, keepdims=True) * inverse[i]
            coef = jnp.where(lane == r, a, coef)
            coef = jnp.where(lane == r + 8, b, coef)
        coef_out[pl.ds(base, chips)] = coef.reshape(chips, 1, lanes)
    along = jnp.sum(unit * slope, axis=-1, keepdims=True)
    grad[...] = ((slope - unit * along) * inv_out).astype(BF16)
    right, left = lax.rem(im + 1, nm), lax.rem(im + nm - 1, nm)

    def cot_copy(i, src, dst, m):
        return pltpu.make_async_remote_copy(
            src_ref=src,
            dst_ref=dst,
            send_sem=cot_sem.at[0, i],
            recv_sem=cot_sem.at[1, i],
            device_id=(ix, iz, ic, m),
            device_id_type=MESH,
        )

    def cot_half(m, i):
        half = quarter // 2
        return cot.at[pl.ds(pl.multiple_of(m * quarter + i * half, half), half), :]

    to_right = cot_copy(0, grad, cot.at[own, :], right)
    to_left = cot_copy(1, grad, cot.at[own, :], left)
    to_right.start()
    to_left.start()
    to_both(lambda core, k: push(coef_out, coef_in, coef_sem, core, chip_at(k)))
    serve_units(1, 0, chips, 1)
    coef_in[me] = coef_out[me]
    cot[own, :] = grad[...]
    to_right.wait_recv()
    on_right = cot_copy(2, cot_half(left, 0), cot_half(left, 0), right)
    on_right.start()
    to_left.wait_recv()
    on_left = cot_copy(3, cot_half(right, 1), cot_half(right, 1), left)
    on_left.start()
    on_right.wait()
    on_left.wait()
    to_right.wait_send()
    to_left.wait_send()

    gated_cot[...] = lax.dot_general(
        cot[...], w_out[...], OVER_COLS, preferred_element_type=F32
    ).astype(BF16)
    for b in range(nm):
        for h in range(heads):
            rows = slice(b * quarter, (b + 1) * quarter)
            cols = slice(h * DH, (h + 1) * DH)
            count = count_ref[rows, :]
            scores, mask, weights, scaled, inv = forward(rows, cols)
            gc = gated_cot[rows, cols].astype(F32)
            d_gating = gc * scaled
            d_scaled = gc * proj[0, rows, cols].astype(F32)
            d_mixed = inv * (
                d_scaled
                - jnp.mean(d_scaled, axis=-1, keepdims=True)
                - scaled * jnp.mean(d_scaled * scaled, axis=-1, keepdims=True)
            )
            d_mixed = d_mixed.astype(BF16)
            d_weights = lax.dot_general(
                d_mixed, proj[1, rows, cols], OVER_COLS, preferred_element_type=F32
            )
            d_weights = d_weights.astype(BF16).astype(F32)
            d_values = lax.dot_general(weights, d_mixed, OVER_ROWS, preferred_element_type=F32)
            d_scores = jnp.where(
                mask, d_weights * silu_slope(scores) * (DH**-0.5) / count, 0.0
            ).astype(BF16)
            d_queries = jnp.dot(d_scores, proj[3, rows, cols], preferred_element_type=F32)
            d_keys = lax.dot_general(
                d_scores, proj[2, rows, cols], OVER_ROWS, preferred_element_type=F32
            )
            for c, d in enumerate((d_gating, d_values, d_queries, d_keys)):
                at = slice(c * cols_here + h * DH, c * cols_here + (h + 1) * DH)
                pre_cot[rows, at] = (
                    d.astype(BF16).astype(F32) * silu_slope(preact[c, rows, cols])
                ).astype(BF16)

    block_rows = width // nx
    groups = parts.shape[0]
    peer_c = (ix, iz, 1 - ic, im)
    swaps = []
    order = [lax.rem(ix + k, nx) for k in list(range(1, nx)) + [0]]
    for i, p in enumerate(order):
        at = pl.ds(pl.multiple_of(p * block_rows, block_rows), block_rows)
        res = lax.dot_general(normed[:, at], pre_cot[...], OVER_ROWS, preferred_element_type=F32)
        for c in range(4):
            parts[c, p] = (
                res[:, c * cols_here : (c + 1) * cols_here].astype(BF16).reshape(parts.shape[2:])
            )
        res = lax.dot_general(cot[:, at], gated[...], OVER_ROWS, preferred_element_type=F32)
        parts[4, p] = res.astype(BF16).reshape(parts.shape[2:])
        swaps.append(
            pltpu.make_async_remote_copy(
                src_ref=parts.at[:, p, :, 1 - ic],
                dst_ref=land_c.at[:, p],
                send_sem=c_sem.at[0, i],
                recv_sem=c_sem.at[1, i],
                device_id=peer_c,
                device_id_type=MESH,
            )
        )
        swaps[-1].start()
    copies = []
    for i in range(nx - 1):
        p = order[i]
        swaps[i].wait()
        stage_x[i] = (parts[:, p, :, ic].astype(F32) + land_c[:, p].astype(F32)).astype(BF16)
        copies.append(
            pltpu.make_async_remote_copy(
                src_ref=stage_x.at[i],
                dst_ref=land_x.at[i],
                send_sem=x_sem.at[0, i],
                recv_sem=x_sem.at[1, i],
                device_id=(p, iz, ic, im),
                device_id_type=MESH,
            )
        )
        copies[-1].start()
    finish(coef_in, coef_sem, 1, n - 1)
    rows_cat = cat.shape[0]
    row = lax.broadcasted_iota(jnp.int32, (chips, rows_cat), 1)
    for p, base in enumerate(bases):
        wanted = asked[pl.ds(base, chips)].reshape(chips, lanes)
        coef = coef_in[pl.ds(base, chips)].reshape(chips, lanes)
        for r in range(CAP):
            b = coef[:, r + 8 : r + 9]
            high = b.astype(BF16).astype(F32)
            span = slice((p * CAP + r) * chips, (p * CAP + r + 1) * chips)
            side[span, :] = jnp.where(
                lane == 0, high, jnp.where(lane == 1, b - high, 0.0)
            ).astype(BF16)
            hot[span, :] = (wanted[:, r : r + 1] == row).astype(F32).astype(BF16)
    both = lax.dot_general(hot[...], side[...], OVER_ROWS, preferred_element_type=F32)
    b_row = both[:, 0:1] + both[:, 1:2]
    for c in range(0, width, 256):
        cat_grad_ref[:, c : c + 256] = -b_row * cat[:, c : c + 256].astype(F32)
    swaps[nx - 1].wait()
    held = parts[:, ix, :, ic].astype(F32) + land_c[:, ix].astype(F32)
    for i, copy in enumerate(copies):
        copy.wait()
        held = held + land_x[i].astype(F32)
    stage_z[...] = held.astype(BF16)
    copies = []
    for i in range(nz - 1):
        p = lax.rem(iz + 1 + i, nz)
        copies.append(
            pltpu.make_async_remote_copy(
                src_ref=stage_z.at[:, p],
                dst_ref=land_z.at[i],
                send_sem=z_sem.at[0, i],
                recv_sem=z_sem.at[1, i],
                device_id=(ix, p, ic, im),
                device_id_type=MESH,
            )
        )
        copies[-1].start()

    def catalogue_half(p):
        base = bases[p]
        finish(unit_in, unit_sem.at[p], 1, chips - 1 + p)
        coef = coef_in[pl.ds(base, chips)].reshape(chips, lanes)
        half = slice(p * CAP * chips, (p + 1) * CAP * chips)
        for r in range(CAP):
            spread(unit_in, base, r)
            a = coef[:, r : r + 1]
            span = slice((p * CAP + r) * chips, (p * CAP + r + 1) * chips)
            for c in range(chunks):
                chunk = tall[pl.ds(c, chips, stride=chunks), :]
                mat[span, c * lanes : (c + 1) * lanes] = (chunk * a).astype(BF16)
        for c in range(0, width, 256):
            at = slice(c, c + 256)
            cat_grad_ref[:, at] += lax.dot_general(
                hot[half, :], mat[half, at], OVER_ROWS, preferred_element_type=F32
            )

    catalogue_half(0)
    catalogue_half(1)
    held = stage_z[:, iz].astype(F32)
    for i, copy in enumerate(copies):
        copy.wait()
        held = held + land_z[i].astype(F32)
    sums_ref[...] = held

    finish(want_out, ids_sem, 0, n - 1)
    finish(hist_out, hist_sem, 0, n_dp - 1)
    for p in range(nc):
        finish(fetch_out, fetch_sem.at[p], 0, chips - 1 + p)
        finish(unit_out, unit_sem.at[p], 0, chips - 1 + p)
    finish(coef_out, coef_sem, 0, n - 1)


ALL = ("x", "z", "c", "mp")
DP = ("x", "z", "c")
NX, NZ, NC, NM = 4, 8, 2, 4
SEQ_DEV = 16


def step(source, lengths, source_2d, owners_t, rows_t, history, catalogue, w_in, w_out):
    n_dp = NX * NZ * NC
    n = n_dp * NM
    seqs, steps, cols = history.shape
    rows_all = seqs * steps
    rows_cat, width = catalogue.shape
    quarter = rows_all // NM
    chunks = width // 128
    rows_out = width // n_dp
    dma = pltpu.SemaphoreType.DMA
    V = pltpu.VMEM
    I32 = jnp.int32
    anyw = pl.BlockSpec(memory_space=pl.ANY)
    message = (n, CAP, chunks, 128)
    scratch = [
        V((rows_all, 1), F32), V((n_dp, 1, 128), I32), pltpu.SMEM((n_dp, 1, 128), I32),
        V(history.shape, BF16), V((n_dp, steps, cols), BF16), V((n_dp, steps, cols), BF16),
        V((rows_cat, chunks, 128), BF16), V(catalogue.shape, BF16), V(w_in.shape, BF16), V(w_out.shape, BF16), dma((4,)),
        V((n, 128), I32), V((n, 128), I32), V((n, quarter), I32), V((n, quarter), I32),
        V((n, 1, 128), I32), V((n, 1, 128), I32), V((n, 1, 128), I32),
        pltpu.SMEM((n, 1, 128), I32), pltpu.SMEM((n, 1, 128), I32), dma((2,)),
        V(message, BF16), V(message, BF16), V(message, BF16), V(message, BF16),
        V((n, 1, 128), F32), V((n, 1, 128), F32),
        V((rows_all, cols), BF16), V((rows_all, width), BF16), V((rows_all, width), BF16),
        V((4, rows_all, cols), F32), V((4, rows_all, cols), BF16), V((rows_all, cols), BF16),
        V((NM - 1, quarter, width), BF16), V((NM - 1, quarter, width), BF16),
        V((quarter, width), F32), V((n // NC * chunks, 128), F32), V((CAP * n, width), BF16),
        V((NC * CAP, n // NC, quarter), F32), V((NC * CAP, n // NC, quarter), F32), V((quarter, width), BF16),
        V((rows_all, width), BF16), V((rows_all, cols), BF16), V((rows_all, 4 * cols), BF16),
        V((5, NX, NZ, NC, rows_out, cols), BF16), V((5, NX, NZ, rows_out, cols), BF16),
        V((NX - 1, 5, NZ, rows_out, cols), BF16), V((NX - 1, 5, NZ, rows_out, cols), BF16),
        V((5, NZ, rows_out, cols), BF16), V((NZ - 1, 5, rows_out, cols), BF16),
        V((CAP * n, rows_cat), BF16), V((CAP * n, 128), BF16),
        dma((2,)), dma((2,)), dma((NC, 2)), dma((NC, 2)), dma((2,)),
        dma((2, NM - 1)), dma((2, NM - 1)), dma((2, 4)),
        dma((2, NX)), dma((2, NX - 1)), dma((2, NZ - 1)),
    ]
    return pl.pallas_call(
        step_kernel,
        out_shape=(sds((rows_cat, width), F32), sds((5, rows_out, cols), F32)),
        in_specs=[SM, SM, VM, VM, VM] + [anyw] * 4,
        out_specs=(VM, VM),
        scratch_shapes=scratch,
        compiler_params=params(collective_id=0, has_side_effects=True),
        name="step",
    )(source, lengths, source_2d, owners_t, rows_t, history, catalogue, w_in, w_out)


def per_device(history, lengths, source, owners, item_rows, catalogue, w_in, w_out):
    cat_grad, sums = step(
        source,
        lengths,
        source.reshape(NX * NZ * NC, SEQ_DEV),
        owners.T,
        item_rows.T,
        history,
        catalogue,
        w_in,
        w_out,
    )
    return (sums[:4], sums[4].T, cat_grad)


def solution(mesh):
    split = Mesh(mesh.devices.reshape(NX, NZ, NC, NM), ALL)
    placed = (
        P(DP, None, "mp"),
        P(),
        P(),
        P(ALL, None),
        P(ALL, None),
        P(ALL, None),
        P(None, None, "mp"),
        P("mp", None),
    )
    return jax.shard_map(
        per_device,
        mesh=split,
        in_specs=placed,
        out_specs=(P(None, DP, "mp"), P("mp", DP), P(ALL, None)),
        check_vma=False,
    )
```

```python
import functools

import jax
import jax.numpy as jnp
from jax import lax
from jax.experimental import pallas as pl
from jax.experimental.pallas import tpu as pltpu
from jax.sharding import Mesh, PartitionSpec as P

DH = 128
CAP = 6
MESH = pl.DeviceIdType.MESH
F32 = jnp.float32
BF16 = jnp.bfloat16

cosine_divisor = 0.05
epsilon_norm = 1e-05
epsilon_unit = 1e-06

VM = pl.BlockSpec(memory_space=pltpu.VMEM)
SM = pl.BlockSpec(memory_space=pltpu.SMEM)


def sds(shape, dtype):
    return jax.ShapeDtypeStruct(shape, dtype)


def params(**kw):
    return pltpu.CompilerParams(vmem_limit_bytes=60 * 1024 * 1024, **kw)


def slots_kernel(own_ref, row_ref, want_ref, event_ref, rank_ref, col_ref):
    owners_n, events = rank_ref.shape
    who = lax.broadcasted_iota(jnp.int32, (owners_n, events), 0)
    named = jnp.zeros((owners_n, events), F32)
    rows = jnp.zeros((owners_n, events), jnp.int32)
    cols = jnp.zeros((owners_n, events), jnp.int32)
    own = own_ref[...]
    core = lax.rem(lax.div(own, NM), NC)
    own = core * (owners_n // NC) + lax.div(own, NM * NC) * NM + lax.rem(own, NM)
    for j in range(own_ref.shape[0]):
        mask = own[j : j + 1, :] == who
        named = jnp.where(mask, 1.0, named)
        rows = jnp.where(mask, row_ref[j : j + 1, :], rows)
        cols = jnp.where(mask, j, cols)
    before = (
        lax.broadcasted_iota(jnp.int32, (events, events), 0)
        < lax.broadcasted_iota(jnp.int32, (events, events), 1)
    ).astype(F32)
    rank = jnp.dot(
        named.astype(BF16), before.astype(BF16), preferred_element_type=F32
    ).astype(jnp.int32)
    rank = jnp.where(named > 0.0, rank, -1)
    rank_ref[...] = rank
    col_ref[...] = cols
    event = lax.broadcasted_iota(jnp.int32, (owners_n, events), 1)
    lane = lax.broadcasted_iota(jnp.int32, want_ref.shape, 1)
    want = jnp.full(want_ref.shape, -1, jnp.int32)
    chosen = jnp.zeros(want_ref.shape, jnp.int32)
    for r in range(CAP):
        here = rank == r
        row_r = jnp.max(jnp.where(here, rows, -1), axis=1, keepdims=True)
        event_r = jnp.max(jnp.where(here, event, 0), axis=1, keepdims=True)
        want = jnp.where(lane == r, row_r, want)
        chosen = jnp.where(lane == r, event_r, chosen)
    want_ref[...] = want
    event_ref[...] = chosen


OVER_ROWS = (((0,), (0,)), ((), ()))
OVER_COLS = (((1,), (1,)), ((), ()))


def sigmoid(v):
    return 1.0 / (1.0 + jnp.exp(-v))


def silu_slope(v):
    s = sigmoid(v)
    return s * (1.0 + v * (1.0 - s))


def center(v):
    moved = v - jnp.mean(v, axis=-1, keepdims=True)
    inv = 1.0 / jnp.sqrt(jnp.mean(moved * moved, axis=-1, keepdims=True) + epsilon_norm)
    return moved * inv, inv


def attention_weights(q, k, count):
    n = q.shape[0]
    scores = lax.dot_general(q, k, OVER_COLS, preferred_element_type=F32) * (DH**-0.5)
    t = lax.broadcasted_iota(jnp.int32, (n, n), 0)
    s = lax.broadcasted_iota(jnp.int32, (n, n), 1)
    first = t - lax.rem(t, STEPS)
    mask = (s >= first) & (s <= t) & ((s - first).astype(F32) < count)
    return scores, mask


STEPS = 32


def step_kernel(
    source_s, lengths_s, source_ref, owners_ref, rows_ref,
    history_hbm, cat_hbm, w_in_hbm, w_out_hbm,
    cat_grad_hbm, sums_ref,
    cat_grad_ref, store_sem, count_ref, seq_v, seq_s, hist, hist_out, arrived, tiles, cat, w_in, w_out, load_sem,
    want, event, rank, col, chosen_v, want_out, asked, asked_s, chosen_s, small_sem,
    fetch_out, fetch_in, unit_out, unit_in, coef_out, coef_in,
    part, flat, normed, preact, proj, gated, staged, landed,
    out_rows, tall, mat, cosine, expo, grad, cot, gated_cot, pre_cot,
    parts, land_c, stage_x, land_x, stage_z, land_z, hot, side,
    ids_sem, hist_sem, fetch_sem, unit_sem, coef_sem, gat_sem, sca_sem, cot_sem,
    c_sem, x_sem, z_sem,
):
    ix, iz, ic, im = (lax.axis_index(a) for a in ALL)
    nx, nz, nc, nm = NX, NZ, NC, NM
    n = nx * nz * nc * nm
    here_dp = (ix * nz + iz) * nc + ic
    n_dp = nx * nz * nc
    chips = nx * nz * nm
    chip = (ix * nz + iz) * nm + im
    me = ic * chips + chip
    cores = (ic, 1 - ic)
    bases = [pl.multiple_of(core * chips, chips) for core in cores]

    def dp_at(d):
        return (lax.div(d, nz * nc), lax.rem(lax.div(d, nc), nz), lax.rem(d, nc))

    def device(core, q):
        return (lax.div(q, nz * nm), lax.rem(lax.div(q, nm), nz), core, lax.rem(q, nm))

    def chip_at(k):
        return lax.rem(chip + k, chips)

    loads = [
        pltpu.make_async_copy(a, b, load_sem.at[i])
        for i, (a, b) in enumerate(
            [(history_hbm, hist), (cat_hbm, cat), (w_in_hbm, w_in), (w_out_hbm, w_out)]
        )
    ]
    for load in loads:
        load.start()

    barrier = pltpu.get_barrier_semaphore()

    def greet(core, k):
        pl.semaphore_signal(
            barrier, inc=1, device_id=device(core, chip_at(k)), device_id_type=MESH
        )

    def to_both(act):
        act(cores[1], 0)
        for core in cores:
            act(core, 1)

        def one(k, carry):
            for core in cores:
                act(core, k)
            return carry

        lax.fori_loop(2, chips, one, 0, unroll=6)

    to_both(greet)

    slots_kernel(owners_ref, rows_ref, want, event, rank, col)
    want_out[...] = want[...].reshape(want_out.shape)
    chosen_v[...] = event[...].reshape(chosen_v.shape)
    to_smem = pltpu.make_async_copy(chosen_v, chosen_s, small_sem.at[0])
    to_smem.start()
    from_here = lax.div(source_ref[...], SEQ_DEV) == here_dp
    local = jnp.where(from_here, lax.rem(source_ref[...], SEQ_DEV), 0)
    groups = 128 // SEQ_DEV
    local = jnp.broadcast_to(
        local.reshape(n_dp // groups, 1, 128), (n_dp // groups, groups, 128)
    ).reshape(n_dp, 128)
    at_row = lax.rem(lax.broadcasted_iota(jnp.int32, (n_dp, 128), 0), groups)
    at_lane = lax.div(lax.broadcasted_iota(jnp.int32, (n_dp, 128), 1), SEQ_DEV)
    local = jnp.max(jnp.where(at_row == at_lane, local, 0), axis=1, keepdims=True)
    seq_v[...] = jnp.broadcast_to(local, (n_dp, 128)).reshape(seq_v.shape)
    seq_copy = pltpu.make_async_copy(seq_v, seq_s, small_sem.at[1])
    seq_copy.start()
    lengths = [lengths_s[source_s[here_dp * SEQ_DEV + i]] for i in range(SEQ_DEV)]
    for i, length in enumerate(lengths):
        count_ref[i * STEPS : (i + 1) * STEPS, :] = jnp.full((STEPS, 1), length).astype(F32)
    loads[0].wait()
    seq_copy.wait()

    def stage(d, carry):
        hist_out[d] = hist[seq_s[d, 0, 0]]
        return carry

    lax.fori_loop(0, n_dp, stage, 0, unroll=4)
    loads[1].wait()
    chunks, lanes = cat.shape[1] // 128, 128
    for i in range(cat.shape[0] // chips):
        rows = slice(i * chips, (i + 1) * chips)
        for c in range(chunks):
            tall[pl.ds(c, chips, stride=chunks), :] = cat[rows, c * lanes : (c + 1) * lanes].astype(F32)
        tiles[rows] = tall[...].reshape(chips, chunks, lanes).astype(BF16)
    pl.semaphore_wait(barrier, n - 1)

    def push(src, dst, sems, core, q):
        pltpu.make_async_remote_copy(
            src_ref=src.at[core * chips + q],
            dst_ref=dst.at[me],
            send_sem=sems.at[0],
            recv_sem=sems.at[1],
            device_id=device(core, q),
            device_id_type=MESH,
        ).start()

    def finish(ref, sems, which, count):
        block = ref.at[pl.ds(0, count)]
        pltpu.make_async_copy(block, block, sems.at[which]).wait()

    to_both(lambda core, k: push(want_out, asked, ids_sem, core, chip_at(k)))
    asked[me] = want_out[me]

    def send_history(k, carry):
        d = lax.rem(here_dp + k, n_dp)
        pltpu.make_async_remote_copy(
            src_ref=hist_out.at[d],
            dst_ref=arrived.at[here_dp],
            send_sem=hist_sem.at[0],
            recv_sem=hist_sem.at[1],
            device_id=dp_at(d) + (im,),
            device_id_type=MESH,
        ).start()
        return carry

    lax.fori_loop(1, n_dp, send_history, 0)
    arrived[here_dp] = hist_out[here_dp]

    to_smem.wait()
    finish(asked, ids_sem, 1, n - 1)
    to_smem = pltpu.make_async_copy(asked, asked_s, small_sem.at[1])
    to_smem.start()
    to_smem.wait()

    def fill(out, d, table, idx):
        for r in range(CAP):
            out[d, r] = table[jnp.maximum(idx[d, 0, r], 0)]

    def serve(out, into, table, idx, sems, core, first, last, unroll):
        fill(out, core * chips + chip_at(first), table, idx)

        def one(k, carry):
            fill(out, core * chips + chip_at(k), table, idx)
            push(out, into, sems, core, chip_at(k - 1))
            return carry

        lax.fori_loop(first + 1, last, one, 0, unroll=unroll)
        push(out, into, sems, core, chip_at(last - 1))

    def serve_rows(part, first, last, unroll):
        serve(fetch_out, fetch_in, tiles, asked_s, fetch_sem.at[part], cores[part], first, last, unroll)

    serve_rows(0, 1, chips, 6)
    fill(fetch_out, me, tiles, asked_s)
    fetch_in[me] = fetch_out[me]

    peers = [lax.rem(im + k, nm) for k in range(1, nm)]
    finish(arrived, hist_sem, 1, n_dp - 1)
    for s in range(SEQ_DEV):
        part[s * STEPS : (s + 1) * STEPS, :] = arrived[lax.div(source_s[here_dp * SEQ_DEV + s], SEQ_DEV)]
    rows_all, cols_here = part.shape
    width = flat.shape[1]
    quarter = rows_all // nm
    mine = pl.ds(pl.multiple_of(im * cols_here, cols_here), cols_here)
    gathers = [
        pltpu.make_async_remote_copy(
            src_ref=part,
            dst_ref=flat.at[:, mine],
            send_sem=gat_sem.at[0, i],
            recv_sem=gat_sem.at[1, i],
            device_id=(ix, iz, ic, p),
            device_id_type=MESH,
        )
        for i, p in enumerate(peers)
    ]
    for copy in gathers:
        copy.start()
    serve_rows(1, 0, chips // 2, 7)
    flat[:, mine] = part[...]
    for copy in gathers:
        copy.wait()

    loads[2].wait()
    loads[3].wait()
    for b in range(nm):
        rows = slice(b * quarter, (b + 1) * quarter)
        scaled, _ = center(flat[rows, :].astype(F32))
        normed[rows, :] = scaled.astype(BF16)
    heads = cols_here // DH
    for c in range(4):
        z = jnp.dot(normed[...], w_in[c], preferred_element_type=F32)
        preact[c] = z
        proj[c] = (z * sigmoid(z)).astype(BF16)

    def forward(rows, cols):
        count = count_ref[rows, :]
        scores, mask = attention_weights(proj[2, rows, cols], proj[3, rows, cols], count)
        weights = jnp.where(mask, scores * sigmoid(scores) / count, 0.0).astype(BF16)
        mixed = jnp.dot(weights, proj[1, rows, cols], preferred_element_type=F32)
        scaled, inv = center(mixed)
        return scores, mask, weights, scaled, inv

    for b in range(nm):
        for h in range(heads):
            rows = slice(b * quarter, (b + 1) * quarter)
            cols = slice(h * DH, (h + 1) * DH)
            scaled = forward(rows, cols)[3]
            gated[rows, cols] = (scaled * proj[0, rows, cols].astype(F32)).astype(BF16)

    def block(m):
        rows = pl.ds(pl.multiple_of(m * quarter, quarter), quarter)
        return jnp.dot(gated[rows, :], w_out[...], preferred_element_type=F32)

    for i, p in enumerate(peers):
        staged[i] = block(p).astype(BF16)
    copies = [
        pltpu.make_async_remote_copy(
            src_ref=staged.at[i],
            dst_ref=landed.at[i],
            send_sem=sca_sem.at[0, i],
            recv_sem=sca_sem.at[1, i],
            device_id=(ix, iz, ic, p),
            device_id_type=MESH,
        )
        for i, p in enumerate(peers)
    ]
    for copy in copies:
        copy.start()
    serve_rows(1, chips // 2, chips, 7)
    own = pl.ds(pl.multiple_of(im * quarter, quarter), quarter)
    total = block(im) + flat[own, :].astype(F32)
    for i, copy in enumerate(copies):
        copy.wait()
        total = total + landed[i].astype(F32)
    out_rows[...] = total
    inv_out = 1.0 / jnp.sqrt(jnp.sum(total * total, axis=-1, keepdims=True) + epsilon_unit)
    unit = total * inv_out
    unit_b = unit.astype(BF16)

    for c in range(chunks):
        tall[pl.ds(c, quarter, stride=chunks), :] = unit[:, c * lanes : (c + 1) * lanes]
    unit_tiles = tiles.at[pl.ds(0, quarter)]
    unit_tiles[...] = tall[...].reshape(quarter, chunks, lanes).astype(BF16)

    def serve_units(part, first, last, unroll):
        serve(unit_out, unit_in, unit_tiles, chosen_s, unit_sem.at[part], cores[part], first, last, unroll)

    serve_units(0, 1, chips, 6)
    fill(unit_out, me, unit_tiles, chosen_s)
    unit_in[me] = unit_out[me]

    def spread(ref, base, r):
        tall[...] = ref[pl.ds(base, chips), r].astype(F32).reshape(chips * chunks, lanes)

    sums = jnp.zeros((1, quarter), F32)
    inverse = {}
    for p, base in enumerate(bases):
        finish(fetch_in, fetch_sem.at[p], 1, chips - 1 + p)
        ranks = rank[pl.ds(base, chips), :]
        for r in range(CAP):
            i = p * CAP + r
            spread(fetch_in, base, r)
            squares = jnp.zeros((chips, lanes), F32)
            for c in range(chunks):
                chunk = tall[pl.ds(c, chips, stride=chunks), :]
                squares = squares + chunk * chunk
                mat[i * chips : (i + 1) * chips, c * lanes : (c + 1) * lanes] = chunk.astype(BF16)
            inv = 1.0 / jnp.sqrt(jnp.sum(squares, axis=-1, keepdims=True) + epsilon_unit)
            inverse[i] = inv
            dots = lax.dot_general(
                mat[i * chips : (i + 1) * chips, :], unit_b, OVER_COLS, preferred_element_type=F32
            )
            cos = dots * inv
            ex = jnp.where(ranks == r, jnp.exp(cos / cosine_divisor), 0.0)
            cosine[i] = cos
            expo[i] = ex
            sums = sums + jnp.sum(ex, axis=0, keepdims=True)
    lane_q = lax.broadcasted_iota(jnp.int32, (1, quarter), 1)
    valid = jnp.zeros((1, quarter), F32)
    for i in range(quarter // STEPS):
        length = lengths_s[source_s[here_dp * SEQ_DEV + im * (quarter // STEPS) + i]]
        inside = (lane_q >= i * STEPS) & (lane_q < (i + 1) * STEPS) & (lane_q - i * STEPS < length)
        valid = jnp.where(inside, 1.0, valid)
    scale = valid / sums
    lane = lax.broadcasted_iota(jnp.int32, (chips, lanes), 1)
    slope = jnp.zeros((quarter, width), F32)
    for p, base in enumerate(bases):
        ranks = rank[pl.ds(base, chips), :]
        first = (col[pl.ds(base, chips), :] == 0).astype(F32) * valid
        coef = jnp.zeros((chips, lanes), F32)
        for r in range(CAP):
            i = p * CAP + r
            share = expo[i] * scale - jnp.where(ranks == r, first, 0.0)
            weight = share * (inverse[i] / cosine_divisor)
            slope = slope + lax.dot_general(
                weight.astype(BF16), mat[i * chips : (i + 1) * chips, :], OVER_ROWS,
                preferred_element_type=F32,
            )
            a = jnp.sum(weight, axis=-1, keepdims=True)
            b = jnp.sum(weight * cosine[i], axis=-1, keepdims=True) * inverse[i]
            coef = jnp.where(lane == r, a, coef)
            coef = jnp.where(lane == r + 8, b, coef)
        coef_out[pl.ds(base, chips)] = coef.reshape(chips, 1, lanes)
    along = jnp.sum(unit * slope, axis=-1, keepdims=True)
    grad[...] = ((slope - unit * along) * inv_out).astype(BF16)
    right, left = lax.rem(im + 1, nm), lax.rem(im + nm - 1, nm)

    def cot_copy(i, src, dst, m):
        return pltpu.make_async_remote_copy(
            src_ref=src,
            dst_ref=dst,
            send_sem=cot_sem.at[0, i],
            recv_sem=cot_sem.at[1, i],
            device_id=(ix, iz, ic, m),
            device_id_type=MESH,
        )

    def cot_half(m, i):
        half = quarter // 2
        return cot.at[pl.ds(pl.multiple_of(m * quarter + i * half, half), half), :]

    to_right = cot_copy(0, grad, cot.at[own, :], right)
    to_left = cot_copy(1, grad, cot.at[own, :], left)
    to_right.start()
    to_left.start()
    to_both(lambda core, k: push(coef_out, coef_in, coef_sem, core, chip_at(k)))
    serve_units(1, 0, chips, 1)
    coef_in[me] = coef_out[me]
    cot[own, :] = grad[...]
    to_right.wait_recv()
    on_right = cot_copy(2, cot_half(left, 0), cot_half(left, 0), right)
    on_right.start()
    to_left.wait_recv()
    on_left = cot_copy(3, cot_half(right, 1), cot_half(right, 1), left)
    on_left.start()
    on_right.wait()
    on_left.wait()
    to_right.wait_send()
    to_left.wait_send()

    gated_cot[...] = lax.dot_general(
        cot[...], w_out[...], OVER_COLS, preferred_element_type=F32
    ).astype(BF16)
    for b in range(nm):
        for h in range(heads):
            rows = slice(b * quarter, (b + 1) * quarter)
            cols = slice(h * DH, (h + 1) * DH)
            count = count_ref[rows, :]
            scores, mask, weights, scaled, inv = forward(rows, cols)
            gc = gated_cot[rows, cols].astype(F32)
            d_gating = gc * scaled
            d_scaled = gc * proj[0, rows, cols].astype(F32)
            d_mixed = inv * (
                d_scaled
                - jnp.mean(d_scaled, axis=-1, keepdims=True)
                - scaled * jnp.mean(d_scaled * scaled, axis=-1, keepdims=True)
            )
            d_mixed = d_mixed.astype(BF16)
            d_weights = lax.dot_general(
                d_mixed, proj[1, rows, cols], OVER_COLS, preferred_element_type=F32
            )
            d_weights = d_weights.astype(BF16).astype(F32)
            d_values = lax.dot_general(weights, d_mixed, OVER_ROWS, preferred_element_type=F32)
            d_scores = jnp.where(
                mask, d_weights * silu_slope(scores) * (DH**-0.5) / count, 0.0
            ).astype(BF16)
            d_queries = jnp.dot(d_scores, proj[3, rows, cols], preferred_element_type=F32)
            d_keys = lax.dot_general(
                d_scores, proj[2, rows, cols], OVER_ROWS, preferred_element_type=F32
            )
            for c, d in enumerate((d_gating, d_values, d_queries, d_keys)):
                at = slice(c * cols_here + h * DH, c * cols_here + (h + 1) * DH)
                pre_cot[rows, at] = (
                    d.astype(BF16).astype(F32) * silu_slope(preact[c, rows, cols])
                ).astype(BF16)

    block_rows = width // nx
    groups = parts.shape[0]
    peer_c = (ix, iz, 1 - ic, im)
    swaps = []
    order = [lax.rem(ix + k, nx) for k in list(range(1, nx)) + [0]]
    for i, p in enumerate(order):
        at = pl.ds(pl.multiple_of(p * block_rows, block_rows), block_rows)
        res = lax.dot_general(normed[:, at], pre_cot[...], OVER_ROWS, preferred_element_type=F32)
        for c in range(4):
            parts[c, p] = (
                res[:, c * cols_here : (c + 1) * cols_here].astype(BF16).reshape(parts.shape[2:])
            )
        res = lax.dot_general(cot[:, at], gated[...], OVER_ROWS, preferred_element_type=F32)
        parts[4, p] = res.astype(BF16).reshape(parts.shape[2:])
        swaps.append(
            pltpu.make_async_remote_copy(
                src_ref=parts.at[:, p, :, 1 - ic],
                dst_ref=land_c.at[:, p],
                send_sem=c_sem.at[0, i],
                recv_sem=c_sem.at[1, i],
                device_id=peer_c,
                device_id_type=MESH,
            )
        )
        swaps[-1].start()
    copies = []
    for i in range(nx - 1):
        p = order[i]
        swaps[i].wait()
        stage_x[i] = (parts[:, p, :, ic].astype(F32) + land_c[:, p].astype(F32)).astype(BF16)
        copies.append(
            pltpu.make_async_remote_copy(
                src_ref=stage_x.at[i],
                dst_ref=land_x.at[i],
                send_sem=x_sem.at[0, i],
                recv_sem=x_sem.at[1, i],
                device_id=(p, iz, ic, im),
                device_id_type=MESH,
            )
        )
        copies[-1].start()
    finish(coef_in, coef_sem, 1, n - 1)
    rows_cat = cat.shape[0]
    row = lax.broadcasted_iota(jnp.int32, (chips, rows_cat), 1)
    for p, base in enumerate(bases):
        wanted = asked[pl.ds(base, chips)].reshape(chips, lanes)
        coef = coef_in[pl.ds(base, chips)].reshape(chips, lanes)
        for r in range(CAP):
            b = coef[:, r + 8 : r + 9]
            high = b.astype(BF16).astype(F32)
            span = slice((p * CAP + r) * chips, (p * CAP + r + 1) * chips)
            side[span, :] = jnp.where(
                lane == 0, high, jnp.where(lane == 1, b - high, 0.0)
            ).astype(BF16)
            hot[span, :] = (wanted[:, r : r + 1] == row).astype(F32).astype(BF16)
    both = lax.dot_general(hot[...], side[...], OVER_ROWS, preferred_element_type=F32)
    b_row = both[:, 0:1] + both[:, 1:2]
    for c in range(0, width, 256):
        cat_grad_ref[:, c : c + 256] = -b_row * cat[:, c : c + 256].astype(F32)
    swaps[nx - 1].wait()
    held = parts[:, ix, :, ic].astype(F32) + land_c[:, ix].astype(F32)
    for i, copy in enumerate(copies):
        copy.wait()
        held = held + land_x[i].astype(F32)
    stage_z[...] = held.astype(BF16)
    copies = []
    for i in range(nz - 1):
        p = lax.rem(iz + 1 + i, nz)
        copies.append(
            pltpu.make_async_remote_copy(
                src_ref=stage_z.at[:, p],
                dst_ref=land_z.at[i],
                send_sem=z_sem.at[0, i],
                recv_sem=z_sem.at[1, i],
                device_id=(ix, p, ic, im),
                device_id_type=MESH,
            )
        )
        copies[-1].start()

    def catalogue_half(p):
        base = bases[p]
        finish(unit_in, unit_sem.at[p], 1, chips - 1 + p)
        coef = coef_in[pl.ds(base, chips)].reshape(chips, lanes)
        half = slice(p * CAP * chips, (p + 1) * CAP * chips)
        for r in range(CAP):
            spread(unit_in, base, r)
            a = coef[:, r : r + 1]
            span = slice((p * CAP + r) * chips, (p * CAP + r + 1) * chips)
            for c in range(chunks):
                chunk = tall[pl.ds(c, chips, stride=chunks), :]
                mat[span, c * lanes : (c + 1) * lanes] = (chunk * a).astype(BF16)
        for c in range(0, width, 256):
            at = slice(c, c + 256)
            cat_grad_ref[:, at] += lax.dot_general(
                hot[half, :], mat[half, at], OVER_ROWS, preferred_element_type=F32
            )

    catalogue_half(0)
    catalogue_half(1)
    store = pltpu.make_async_copy(cat_grad_ref, cat_grad_hbm, store_sem)
    store.start()
    held = stage_z[:, iz].astype(F32)
    for i, copy in enumerate(copies):
        copy.wait()
        held = held + land_z[i].astype(F32)
    sums_ref[...] = held

    store.wait()
    finish(want_out, ids_sem, 0, n - 1)
    finish(hist_out, hist_sem, 0, n_dp - 1)
    for p in range(nc):
        finish(fetch_out, fetch_sem.at[p], 0, chips - 1 + p)
        finish(unit_out, unit_sem.at[p], 0, chips - 1 + p)
    finish(coef_out, coef_sem, 0, n - 1)


ALL = ("x", "z", "c", "mp")
DP = ("x", "z", "c")
NX, NZ, NC, NM = 4, 8, 2, 4
SEQ_DEV = 16


def step(source, lengths, source_2d, owners_t, rows_t, history, catalogue, w_in, w_out):
    n_dp = NX * NZ * NC
    n = n_dp * NM
    seqs, steps, cols = history.shape
    rows_all = seqs * steps
    rows_cat, width = catalogue.shape
    quarter = rows_all // NM
    chunks = width // 128
    rows_out = width // n_dp
    dma = pltpu.SemaphoreType.DMA
    V = pltpu.VMEM
    I32 = jnp.int32
    anyw = pl.BlockSpec(memory_space=pl.ANY)
    message = (n, CAP, chunks, 128)
    scratch = [
        V((rows_cat, width), F32), dma, V((rows_all, 1), F32), V((n_dp, 1, 128), I32), pltpu.SMEM((n_dp, 1, 128), I32),
        V(history.shape, BF16), V((n_dp, steps, cols), BF16), V((n_dp, steps, cols), BF16),
        V((rows_cat, chunks, 128), BF16), V(catalogue.shape, BF16), V(w_in.shape, BF16), V(w_out.shape, BF16), dma((4,)),
        V((n, 128), I32), V((n, 128), I32), V((n, quarter), I32), V((n, quarter), I32),
        V((n, 1, 128), I32), V((n, 1, 128), I32), V((n, 1, 128), I32),
        pltpu.SMEM((n, 1, 128), I32), pltpu.SMEM((n, 1, 128), I32), dma((2,)),
        V(message, BF16), V(message, BF16), V(message, BF16), V(message, BF16),
        V((n, 1, 128), F32), V((n, 1, 128), F32),
        V((rows_all, cols), BF16), V((rows_all, width), BF16), V((rows_all, width), BF16),
        V((4, rows_all, cols), F32), V((4, rows_all, cols), BF16), V((rows_all, cols), BF16),
        V((NM - 1, quarter, width), BF16), V((NM - 1, quarter, width), BF16),
        V((quarter, width), F32), V((n // NC * chunks, 128), F32), V((CAP * n, width), BF16),
        V((NC * CAP, n // NC, quarter), F32), V((NC * CAP, n // NC, quarter), F32), V((quarter, width), BF16),
        V((rows_all, width), BF16), V((rows_all, cols), BF16), V((rows_all, 4 * cols), BF16),
        V((5, NX, NZ, NC, rows_out, cols), BF16), V((5, NX, NZ, rows_out, cols), BF16),
        V((NX - 1, 5, NZ, rows_out, cols), BF16), V((NX - 1, 5, NZ, rows_out, cols), BF16),
        V((5, NZ, rows_out, cols), BF16), V((NZ - 1, 5, rows_out, cols), BF16),
        V((CAP * n, rows_cat), BF16), V((CAP * n, 128), BF16),
        dma((2,)), dma((2,)), dma((NC, 2)), dma((NC, 2)), dma((2,)),
        dma((2, NM - 1)), dma((2, NM - 1)), dma((2, 4)),
        dma((2, NX)), dma((2, NX - 1)), dma((2, NZ - 1)),
    ]
    return pl.pallas_call(
        step_kernel,
        out_shape=(sds((rows_cat, width), F32), sds((5, rows_out, cols), F32)),
        in_specs=[SM, SM, VM, VM, VM] + [anyw] * 4,
        out_specs=(anyw, VM),
        scratch_shapes=scratch,
        compiler_params=params(collective_id=0, has_side_effects=True),
        name="step",
    )(source, lengths, source_2d, owners_t, rows_t, history, catalogue, w_in, w_out)


def per_device(history, lengths, source, owners, item_rows, catalogue, w_in, w_out):
    cat_grad, sums = step(
        source,
        lengths,
        source.reshape(-1, 128),
        owners.T,
        item_rows.T,
        history,
        catalogue,
        w_in,
        w_out,
    )
    return (sums[:4], sums[4].T, cat_grad)


def solution(mesh):
    split = Mesh(mesh.devices.reshape(NX, NZ, NC, NM), ALL)
    placed = (
        P(DP, None, "mp"),
        P(),
        P(),
        P(ALL, None),
        P(ALL, None),
        P(ALL, None),
        P(None, None, "mp"),
        P("mp", None),
    )
    return jax.shard_map(
        per_device,
        mesh=split,
        in_specs=placed,
        out_specs=(P(None, DP, "mp"), P("mp", DP), P(ALL, None)),
        check_vma=False,
    )
```

```python
import functools

import jax
import jax.numpy as jnp
from jax import lax
from jax.experimental import pallas as pl
from jax.experimental.pallas import tpu as pltpu
from jax.sharding import Mesh, PartitionSpec as P

DH = 128
CAP = 6
MESH = pl.DeviceIdType.MESH
F32 = jnp.float32
BF16 = jnp.bfloat16

cosine_divisor = 0.05
epsilon_norm = 1e-05
epsilon_unit = 1e-06

VM = pl.BlockSpec(memory_space=pltpu.VMEM)
SM = pl.BlockSpec(memory_space=pltpu.SMEM)


def sds(shape, dtype):
    return jax.ShapeDtypeStruct(shape, dtype)


def params(**kw):
    return pltpu.CompilerParams(vmem_limit_bytes=60 * 1024 * 1024, **kw)


def slots_kernel(own_ref, row_ref, want_ref, event_ref, rank_ref, col_ref):
    owners_n, events = rank_ref.shape
    who = lax.broadcasted_iota(jnp.int32, (owners_n, events), 0)
    named = jnp.zeros((owners_n, events), F32)
    rows = jnp.zeros((owners_n, events), jnp.int32)
    cols = jnp.zeros((owners_n, events), jnp.int32)
    own = own_ref[...]
    core = lax.rem(lax.div(own, NM), NC)
    own = core * (owners_n // NC) + lax.div(own, NM * NC) * NM + lax.rem(own, NM)
    for j in range(own_ref.shape[0]):
        mask = own[j : j + 1, :] == who
        named = jnp.where(mask, 1.0, named)
        rows = jnp.where(mask, row_ref[j : j + 1, :], rows)
        cols = jnp.where(mask, j, cols)
    before = (
        lax.broadcasted_iota(jnp.int32, (events, events), 0)
        < lax.broadcasted_iota(jnp.int32, (events, events), 1)
    ).astype(F32)
    rank = jnp.dot(
        named.astype(BF16), before.astype(BF16), preferred_element_type=F32
    ).astype(jnp.int32)
    rank = jnp.where(named > 0.0, rank, -1)
    rank_ref[...] = rank
    col_ref[...] = cols
    event = lax.broadcasted_iota(jnp.int32, (owners_n, events), 1)
    lane = lax.broadcasted_iota(jnp.int32, want_ref.shape, 1)
    want = jnp.full(want_ref.shape, -1, jnp.int32)
    chosen = jnp.zeros(want_ref.shape, jnp.int32)
    for r in range(CAP):
        here = rank == r
        row_r = jnp.max(jnp.where(here, rows, -1), axis=1, keepdims=True)
        event_r = jnp.max(jnp.where(here, event, 0), axis=1, keepdims=True)
        want = jnp.where(lane == r, row_r, want)
        chosen = jnp.where(lane == r, event_r, chosen)
    want_ref[...] = want
    event_ref[...] = chosen


OVER_ROWS = (((0,), (0,)), ((), ()))
OVER_COLS = (((1,), (1,)), ((), ()))


def sigmoid(v):
    return 1.0 / (1.0 + jnp.exp(-v))


def silu_slope(v):
    s = sigmoid(v)
    return s * (1.0 + v * (1.0 - s))


def center(v):
    moved = v - jnp.mean(v, axis=-1, keepdims=True)
    inv = 1.0 / jnp.sqrt(jnp.mean(moved * moved, axis=-1, keepdims=True) + epsilon_norm)
    return moved * inv, inv


def attention_weights(q, k, count):
    n = q.shape[0]
    scores = lax.dot_general(q, k, OVER_COLS, preferred_element_type=F32) * (DH**-0.5)
    t = lax.broadcasted_iota(jnp.int32, (n, n), 0)
    s = lax.broadcasted_iota(jnp.int32, (n, n), 1)
    first = t - lax.rem(t, STEPS)
    mask = (s >= first) & (s <= t) & ((s - first).astype(F32) < count)
    return scores, mask


STEPS = 32


def step_kernel(
    source_s, lengths_s, source_ref, owners_ref, rows_ref,
    history_hbm, cat_hbm, w_in_hbm, w_out_hbm,
    cat_grad_hbm, w_in_sum, w_out_sum,
    cat_grad_ref, store_sem, count_ref, seq_v, seq_s, hist, hist_out, arrived, tiles, cat, w_in, w_out, load_sem,
    want, event, rank, col, chosen_v, want_out, asked, asked_s, chosen_s, small_sem,
    fetch_out, fetch_in, unit_out, unit_in, coef_out, coef_in,
    part, flat, normed, preact, proj, gated, staged, landed,
    out_rows, tall, mat, cosine, expo, grad, cot, gated_cot, pre_cot,
    parts, land_c, stage_x, land_x, stage_z, land_z, hot, side,
    ids_sem, hist_sem, fetch_sem, unit_sem, coef_sem, gat_sem, sca_sem, cot_sem,
    c_sem, x_sem, z_sem,
):
    ix, iz, ic, im = (lax.axis_index(a) for a in ALL)
    nx, nz, nc, nm = NX, NZ, NC, NM
    n = nx * nz * nc * nm
    here_dp = (ix * nz + iz) * nc + ic
    n_dp = nx * nz * nc
    chips = nx * nz * nm
    chip = (ix * nz + iz) * nm + im
    me = ic * chips + chip
    cores = (ic, 1 - ic)
    bases = [pl.multiple_of(core * chips, chips) for core in cores]

    def dp_at(d):
        return (lax.div(d, nz * nc), lax.rem(lax.div(d, nc), nz), lax.rem(d, nc))

    def device(core, q):
        return (lax.div(q, nz * nm), lax.rem(lax.div(q, nm), nz), core, lax.rem(q, nm))

    def chip_at(k):
        return lax.rem(chip + k, chips)

    loads = [
        pltpu.make_async_copy(a, b, load_sem.at[i])
        for i, (a, b) in enumerate(
            [(history_hbm, hist), (cat_hbm, cat), (w_in_hbm, w_in), (w_out_hbm, w_out)]
        )
    ]
    for load in loads:
        load.start()

    barrier = pltpu.get_barrier_semaphore()

    def greet(core, k):
        pl.semaphore_signal(
            barrier, inc=1, device_id=device(core, chip_at(k)), device_id_type=MESH
        )

    def to_both(act):
        act(cores[1], 0)
        for core in cores:
            act(core, 1)

        def one(k, carry):
            for core in cores:
                act(core, k)
            return carry

        lax.fori_loop(2, chips, one, 0, unroll=6)

    to_both(greet)

    slots_kernel(owners_ref, rows_ref, want, event, rank, col)
    want_out[...] = want[...].reshape(want_out.shape)
    chosen_v[...] = event[...].reshape(chosen_v.shape)
    to_smem = pltpu.make_async_copy(chosen_v, chosen_s, small_sem.at[0])
    to_smem.start()
    from_here = lax.div(source_ref[...], SEQ_DEV) == here_dp
    local = jnp.where(from_here, lax.rem(source_ref[...], SEQ_DEV), 0)
    groups = 128 // SEQ_DEV
    local = jnp.broadcast_to(
        local.reshape(n_dp // groups, 1, 128), (n_dp // groups, groups, 128)
    ).reshape(n_dp, 128)
    at_row = lax.rem(lax.broadcasted_iota(jnp.int32, (n_dp, 128), 0), groups)
    at_lane = lax.div(lax.broadcasted_iota(jnp.int32, (n_dp, 128), 1), SEQ_DEV)
    local = jnp.max(jnp.where(at_row == at_lane, local, 0), axis=1, keepdims=True)
    seq_v[...] = jnp.broadcast_to(local, (n_dp, 128)).reshape(seq_v.shape)
    seq_copy = pltpu.make_async_copy(seq_v, seq_s, small_sem.at[1])
    seq_copy.start()
    lengths = [lengths_s[source_s[here_dp * SEQ_DEV + i]] for i in range(SEQ_DEV)]
    for i, length in enumerate(lengths):
        count_ref[i * STEPS : (i + 1) * STEPS, :] = jnp.full((STEPS, 1), length).astype(F32)
    loads[0].wait()
    seq_copy.wait()

    def stage(d, carry):
        hist_out[d] = hist[seq_s[d, 0, 0]]
        return carry

    lax.fori_loop(0, n_dp, stage, 0, unroll=4)
    loads[1].wait()
    chunks, lanes = cat.shape[1] // 128, 128
    for i in range(cat.shape[0] // chips):
        rows = slice(i * chips, (i + 1) * chips)
        for c in range(chunks):
            tall[pl.ds(c, chips, stride=chunks), :] = cat[rows, c * lanes : (c + 1) * lanes].astype(F32)
        tiles[rows] = tall[...].reshape(chips, chunks, lanes).astype(BF16)
    pl.semaphore_wait(barrier, n - 1)

    def push(src, dst, sems, core, q):
        pltpu.make_async_remote_copy(
            src_ref=src.at[core * chips + q],
            dst_ref=dst.at[me],
            send_sem=sems.at[0],
            recv_sem=sems.at[1],
            device_id=device(core, q),
            device_id_type=MESH,
        ).start()

    def finish(ref, sems, which, count):
        block = ref.at[pl.ds(0, count)]
        pltpu.make_async_copy(block, block, sems.at[which]).wait()

    to_both(lambda core, k: push(want_out, asked, ids_sem, core, chip_at(k)))
    asked[me] = want_out[me]

    def send_history(k, carry):
        d = lax.rem(here_dp + k, n_dp)
        pltpu.make_async_remote_copy(
            src_ref=hist_out.at[d],
            dst_ref=arrived.at[here_dp],
            send_sem=hist_sem.at[0],
            recv_sem=hist_sem.at[1],
            device_id=dp_at(d) + (im,),
            device_id_type=MESH,
        ).start()
        return carry

    lax.fori_loop(1, n_dp, send_history, 0)
    arrived[here_dp] = hist_out[here_dp]

    to_smem.wait()
    finish(asked, ids_sem, 1, n - 1)
    to_smem = pltpu.make_async_copy(asked, asked_s, small_sem.at[1])
    to_smem.start()
    to_smem.wait()

    def fill(out, d, table, idx):
        for r in range(CAP):
            out[d, r] = table[jnp.maximum(idx[d, 0, r], 0)]

    def serve(out, into, table, idx, sems, core, first, last, unroll):
        fill(out, core * chips + chip_at(first), table, idx)

        def one(k, carry):
            fill(out, core * chips + chip_at(k), table, idx)
            push(out, into, sems, core, chip_at(k - 1))
            return carry

        lax.fori_loop(first + 1, last, one, 0, unroll=unroll)
        push(out, into, sems, core, chip_at(last - 1))

    def serve_rows(part, first, last, unroll):
        serve(fetch_out, fetch_in, tiles, asked_s, fetch_sem.at[part], cores[part], first, last, unroll)

    serve_rows(0, 1, chips, 6)
    fill(fetch_out, me, tiles, asked_s)
    fetch_in[me] = fetch_out[me]

    peers = [lax.rem(im + k, nm) for k in range(1, nm)]
    finish(arrived, hist_sem, 1, n_dp - 1)
    for s in range(SEQ_DEV):
        part[s * STEPS : (s + 1) * STEPS, :] = arrived[lax.div(source_s[here_dp * SEQ_DEV + s], SEQ_DEV)]
    rows_all, cols_here = part.shape
    width = flat.shape[1]
    quarter = rows_all // nm
    mine = pl.ds(pl.multiple_of(im * cols_here, cols_here), cols_here)
    gathers = [
        pltpu.make_async_remote_copy(
            src_ref=part,
            dst_ref=flat.at[:, mine],
            send_sem=gat_sem.at[0, i],
            recv_sem=gat_sem.at[1, i],
            device_id=(ix, iz, ic, p),
            device_id_type=MESH,
        )
        for i, p in enumerate(peers)
    ]
    for copy in gathers:
        copy.start()
    serve_rows(1, 0, chips // 2, 7)
    flat[:, mine] = part[...]
    for copy in gathers:
        copy.wait()

    loads[2].wait()
    loads[3].wait()
    for b in range(nm):
        rows = slice(b * quarter, (b + 1) * quarter)
        scaled, _ = center(flat[rows, :].astype(F32))
        normed[rows, :] = scaled.astype(BF16)
    heads = cols_here // DH
    for c in range(4):
        z = jnp.dot(normed[...], w_in[c], preferred_element_type=F32)
        preact[c] = z
        proj[c] = (z * sigmoid(z)).astype(BF16)

    def forward(rows, cols):
        count = count_ref[rows, :]
        scores, mask = attention_weights(proj[2, rows, cols], proj[3, rows, cols], count)
        weights = jnp.where(mask, scores * sigmoid(scores) / count, 0.0).astype(BF16)
        mixed = jnp.dot(weights, proj[1, rows, cols], preferred_element_type=F32)
        scaled, inv = center(mixed)
        return scores, mask, weights, scaled, inv

    for b in range(nm):
        for h in range(heads):
            rows = slice(b * quarter, (b + 1) * quarter)
            cols = slice(h * DH, (h + 1) * DH)
            scaled = forward(rows, cols)[3]
            gated[rows, cols] = (scaled * proj[0, rows, cols].astype(F32)).astype(BF16)

    def block(m):
        rows = pl.ds(pl.multiple_of(m * quarter, quarter), quarter)
        return jnp.dot(gated[rows, :], w_out[...], preferred_element_type=F32)

    for i, p in enumerate(peers):
        staged[i] = block(p).astype(BF16)
    copies = [
        pltpu.make_async_remote_copy(
            src_ref=staged.at[i],
            dst_ref=landed.at[i],
            send_sem=sca_sem.at[0, i],
            recv_sem=sca_sem.at[1, i],
            device_id=(ix, iz, ic, p),
            device_id_type=MESH,
        )
        for i, p in enumerate(peers)
    ]
    for copy in copies:
        copy.start()
    serve_rows(1, chips // 2, chips, 7)
    own = pl.ds(pl.multiple_of(im * quarter, quarter), quarter)
    total = block(im) + flat[own, :].astype(F32)
    for i, copy in enumerate(copies):
        copy.wait()
        total = total + landed[i].astype(F32)
    out_rows[...] = total
    inv_out = 1.0 / jnp.sqrt(jnp.sum(total * total, axis=-1, keepdims=True) + epsilon_unit)
    unit = total * inv_out
    unit_b = unit.astype(BF16)

    for c in range(chunks):
        tall[pl.ds(c, quarter, stride=chunks), :] = unit[:, c * lanes : (c + 1) * lanes]
    unit_tiles = tiles.at[pl.ds(0, quarter)]
    unit_tiles[...] = tall[...].reshape(quarter, chunks, lanes).astype(BF16)

    def serve_units(part, first, last, unroll):
        serve(unit_out, unit_in, unit_tiles, chosen_s, unit_sem.at[part], cores[part], first, last, unroll)

    serve_units(0, 1, chips, 6)
    fill(unit_out, me, unit_tiles, chosen_s)
    unit_in[me] = unit_out[me]

    def spread(ref, base, r):
        tall[...] = ref[pl.ds(base, chips), r].astype(F32).reshape(chips * chunks, lanes)

    sums = jnp.zeros((1, quarter), F32)
    inverse = {}
    for p, base in enumerate(bases):
        finish(fetch_in, fetch_sem.at[p], 1, chips - 1 + p)
        ranks = rank[pl.ds(base, chips), :]
        for r in range(CAP):
            i = p * CAP + r
            spread(fetch_in, base, r)
            squares = jnp.zeros((chips, lanes), F32)
            for c in range(chunks):
                chunk = tall[pl.ds(c, chips, stride=chunks), :]
                squares = squares + chunk * chunk
                mat[i * chips : (i + 1) * chips, c * lanes : (c + 1) * lanes] = chunk.astype(BF16)
            inv = 1.0 / jnp.sqrt(jnp.sum(squares, axis=-1, keepdims=True) + epsilon_unit)
            inverse[i] = inv
            dots = lax.dot_general(
                mat[i * chips : (i + 1) * chips, :], unit_b, OVER_COLS, preferred_element_type=F32
            )
            cos = dots * inv
            ex = jnp.where(ranks == r, jnp.exp(cos / cosine_divisor), 0.0)
            cosine[i] = cos
            expo[i] = ex
            sums = sums + jnp.sum(ex, axis=0, keepdims=True)
    lane_q = lax.broadcasted_iota(jnp.int32, (1, quarter), 1)
    valid = jnp.zeros((1, quarter), F32)
    for i in range(quarter // STEPS):
        length = lengths_s[source_s[here_dp * SEQ_DEV + im * (quarter // STEPS) + i]]
        inside = (lane_q >= i * STEPS) & (lane_q < (i + 1) * STEPS) & (lane_q - i * STEPS < length)
        valid = jnp.where(inside, 1.0, valid)
    scale = valid / sums
    lane = lax.broadcasted_iota(jnp.int32, (chips, lanes), 1)
    slope = jnp.zeros((quarter, width), F32)
    for p, base in enumerate(bases):
        ranks = rank[pl.ds(base, chips), :]
        first = (col[pl.ds(base, chips), :] == 0).astype(F32) * valid
        coef = jnp.zeros((chips, lanes), F32)
        for r in range(CAP):
            i = p * CAP + r
            share = expo[i] * scale - jnp.where(ranks == r, first, 0.0)
            weight = share * (inverse[i] / cosine_divisor)
            slope = slope + lax.dot_general(
                weight.astype(BF16), mat[i * chips : (i + 1) * chips, :], OVER_ROWS,
                preferred_element_type=F32,
            )
            a = jnp.sum(weight, axis=-1, keepdims=True)
            b = jnp.sum(weight * cosine[i], axis=-1, keepdims=True) * inverse[i]
            coef = jnp.where(lane == r, a, coef)
            coef = jnp.where(lane == r + 8, b, coef)
        coef_out[pl.ds(base, chips)] = coef.reshape(chips, 1, lanes)
    along = jnp.sum(unit * slope, axis=-1, keepdims=True)
    grad[...] = ((slope - unit * along) * inv_out).astype(BF16)
    right, left = lax.rem(im + 1, nm), lax.rem(im + nm - 1, nm)

    def cot_copy(i, src, dst, m):
        return pltpu.make_async_remote_copy(
            src_ref=src,
            dst_ref=dst,
            send_sem=cot_sem.at[0, i],
            recv_sem=cot_sem.at[1, i],
            device_id=(ix, iz, ic, m),
            device_id_type=MESH,
        )

    def cot_half(m, i):
        half = quarter // 2
        return cot.at[pl.ds(pl.multiple_of(m * quarter + i * half, half), half), :]

    to_right = cot_copy(0, grad, cot.at[own, :], right)
    to_left = cot_copy(1, grad, cot.at[own, :], left)
    to_right.start()
    to_left.start()
    to_both(lambda core, k: push(coef_out, coef_in, coef_sem, core, chip_at(k)))
    serve_units(1, 0, chips, 1)
    coef_in[me] = coef_out[me]
    cot[own, :] = grad[...]
    to_right.wait_recv()
    on_right = cot_copy(2, cot_half(left, 0), cot_half(left, 0), right)
    on_right.start()
    to_left.wait_recv()
    on_left = cot_copy(3, cot_half(right, 1), cot_half(right, 1), left)
    on_left.start()
    on_right.wait()
    on_left.wait()
    to_right.wait_send()
    to_left.wait_send()

    gated_cot[...] = lax.dot_general(
        cot[...], w_out[...], OVER_COLS, preferred_element_type=F32
    ).astype(BF16)
    for b in range(nm):
        for h in range(heads):
            rows = slice(b * quarter, (b + 1) * quarter)
            cols = slice(h * DH, (h + 1) * DH)
            count = count_ref[rows, :]
            scores, mask, weights, scaled, inv = forward(rows, cols)
            gc = gated_cot[rows, cols].astype(F32)
            d_gating = gc * scaled
            d_scaled = gc * proj[0, rows, cols].astype(F32)
            d_mixed = inv * (
                d_scaled
                - jnp.mean(d_scaled, axis=-1, keepdims=True)
                - scaled * jnp.mean(d_scaled * scaled, axis=-1, keepdims=True)
            )
            d_mixed = d_mixed.astype(BF16)
            d_weights = lax.dot_general(
                d_mixed, proj[1, rows, cols], OVER_COLS, preferred_element_type=F32
            )
            d_weights = d_weights.astype(BF16).astype(F32)
            d_values = lax.dot_general(weights, d_mixed, OVER_ROWS, preferred_element_type=F32)
            d_scores = jnp.where(
                mask, d_weights * silu_slope(scores) * (DH**-0.5) / count, 0.0
            ).astype(BF16)
            d_queries = jnp.dot(d_scores, proj[3, rows, cols], preferred_element_type=F32)
            d_keys = lax.dot_general(
                d_scores, proj[2, rows, cols], OVER_ROWS, preferred_element_type=F32
            )
            for c, d in enumerate((d_gating, d_values, d_queries, d_keys)):
                at = slice(c * cols_here + h * DH, c * cols_here + (h + 1) * DH)
                pre_cot[rows, at] = (
                    d.astype(BF16).astype(F32) * silu_slope(preact[c, rows, cols])
                ).astype(BF16)

    block_rows = width // nx
    groups = parts.shape[0]
    peer_c = (ix, iz, 1 - ic, im)
    swaps = []
    order = [lax.rem(ix + k, nx) for k in list(range(1, nx)) + [0]]
    for i, p in enumerate(order):
        at = pl.ds(pl.multiple_of(p * block_rows, block_rows), block_rows)
        res = lax.dot_general(normed[:, at], pre_cot[...], OVER_ROWS, preferred_element_type=F32)
        for c in range(4):
            parts[c, p] = (
                res[:, c * cols_here : (c + 1) * cols_here].astype(BF16).reshape(parts.shape[2:])
            )
        res = lax.dot_general(cot[:, at], gated[...], OVER_ROWS, preferred_element_type=F32)
        parts[4, p] = res.astype(BF16).reshape(parts.shape[2:])
        swaps.append(
            pltpu.make_async_remote_copy(
                src_ref=parts.at[:, p, :, 1 - ic],
                dst_ref=land_c.at[:, p],
                send_sem=c_sem.at[0, i],
                recv_sem=c_sem.at[1, i],
                device_id=peer_c,
                device_id_type=MESH,
            )
        )
        swaps[-1].start()
    copies = []
    for i in range(nx - 1):
        p = order[i]
        swaps[i].wait()
        stage_x[i] = (parts[:, p, :, ic].astype(F32) + land_c[:, p].astype(F32)).astype(BF16)
        copies.append(
            pltpu.make_async_remote_copy(
                src_ref=stage_x.at[i],
                dst_ref=land_x.at[i],
                send_sem=x_sem.at[0, i],
                recv_sem=x_sem.at[1, i],
                device_id=(p, iz, ic, im),
                device_id_type=MESH,
            )
        )
        copies[-1].start()
    finish(coef_in, coef_sem, 1, n - 1)
    rows_cat = cat.shape[0]
    row = lax.broadcasted_iota(jnp.int32, (chips, rows_cat), 1)
    for p, base in enumerate(bases):
        wanted = asked[pl.ds(base, chips)].reshape(chips, lanes)
        coef = coef_in[pl.ds(base, chips)].reshape(chips, lanes)
        for r in range(CAP):
            b = coef[:, r + 8 : r + 9]
            high = b.astype(BF16).astype(F32)
            span = slice((p * CAP + r) * chips, (p * CAP + r + 1) * chips)
            side[span, :] = jnp.where(
                lane == 0, high, jnp.where(lane == 1, b - high, 0.0)
            ).astype(BF16)
            hot[span, :] = (wanted[:, r : r + 1] == row).astype(F32).astype(BF16)
    both = lax.dot_general(hot[...], side[...], OVER_ROWS, preferred_element_type=F32)
    b_row = both[:, 0:1] + both[:, 1:2]
    for c in range(0, width, 256):
        cat_grad_ref[:, c : c + 256] = -b_row * cat[:, c : c + 256].astype(F32)
    swaps[nx - 1].wait()
    held = parts[:, ix, :, ic].astype(F32) + land_c[:, ix].astype(F32)
    for i, copy in enumerate(copies):
        copy.wait()
        held = held + land_x[i].astype(F32)
    stage_z[...] = held.astype(BF16)
    copies = []
    for i in range(nz - 1):
        p = lax.rem(iz + 1 + i, nz)
        copies.append(
            pltpu.make_async_remote_copy(
                src_ref=stage_z.at[:, p],
                dst_ref=land_z.at[i],
                send_sem=z_sem.at[0, i],
                recv_sem=z_sem.at[1, i],
                device_id=(ix, p, ic, im),
                device_id_type=MESH,
            )
        )
        copies[-1].start()

    def catalogue_half(p):
        base = bases[p]
        finish(unit_in, unit_sem.at[p], 1, chips - 1 + p)
        coef = coef_in[pl.ds(base, chips)].reshape(chips, lanes)
        half = slice(p * CAP * chips, (p + 1) * CAP * chips)
        for r in range(CAP):
            spread(unit_in, base, r)
            a = coef[:, r : r + 1]
            span = slice((p * CAP + r) * chips, (p * CAP + r + 1) * chips)
            for c in range(chunks):
                chunk = tall[pl.ds(c, chips, stride=chunks), :]
                mat[span, c * lanes : (c + 1) * lanes] = (chunk * a).astype(BF16)
        for c in range(0, width, 256):
            at = slice(c, c + 256)
            cat_grad_ref[:, at] += lax.dot_general(
                hot[half, :], mat[half, at], OVER_ROWS, preferred_element_type=F32
            )

    catalogue_half(0)
    catalogue_half(1)
    store = pltpu.make_async_copy(cat_grad_ref, cat_grad_hbm, store_sem)
    store.start()
    held = stage_z[:, iz].astype(F32)
    for i, copy in enumerate(copies):
        copy.wait()
        held = held + land_z[i].astype(F32)
    w_in_sum[...] = held[:4]
    w_out_sum[...] = held[4]

    store.wait()
    finish(want_out, ids_sem, 0, n - 1)
    finish(hist_out, hist_sem, 0, n_dp - 1)
    for p in range(nc):
        finish(fetch_out, fetch_sem.at[p], 0, chips - 1 + p)
        finish(unit_out, unit_sem.at[p], 0, chips - 1 + p)
    finish(coef_out, coef_sem, 0, n - 1)


ALL = ("x", "z", "c", "mp")
DP = ("x", "z", "c")
NX, NZ, NC, NM = 4, 8, 2, 4
SEQ_DEV = 16


def step(source, lengths, source_2d, owners_t, rows_t, history, catalogue, w_in, w_out):
    n_dp = NX * NZ * NC
    n = n_dp * NM
    seqs, steps, cols = history.shape
    rows_all = seqs * steps
    rows_cat, width = catalogue.shape
    quarter = rows_all // NM
    chunks = width // 128
    rows_out = width // n_dp
    dma = pltpu.SemaphoreType.DMA
    V = pltpu.VMEM
    I32 = jnp.int32
    anyw = pl.BlockSpec(memory_space=pl.ANY)
    message = (n, CAP, chunks, 128)
    scratch = [
        V((rows_cat, width), F32), dma, V((rows_all, 1), F32), V((n_dp, 1, 128), I32), pltpu.SMEM((n_dp, 1, 128), I32),
        V(history.shape, BF16), V((n_dp, steps, cols), BF16), V((n_dp, steps, cols), BF16),
        V((rows_cat, chunks, 128), BF16), V(catalogue.shape, BF16), V(w_in.shape, BF16), V(w_out.shape, BF16), dma((4,)),
        V((n, 128), I32), V((n, 128), I32), V((n, quarter), I32), V((n, quarter), I32),
        V((n, 1, 128), I32), V((n, 1, 128), I32), V((n, 1, 128), I32),
        pltpu.SMEM((n, 1, 128), I32), pltpu.SMEM((n, 1, 128), I32), dma((2,)),
        V(message, BF16), V(message, BF16), V(message, BF16), V(message, BF16),
        V((n, 1, 128), F32), V((n, 1, 128), F32),
        V((rows_all, cols), BF16), V((rows_all, width), BF16), V((rows_all, width), BF16),
        V((4, rows_all, cols), F32), V((4, rows_all, cols), BF16), V((rows_all, cols), BF16),
        V((NM - 1, quarter, width), BF16), V((NM - 1, quarter, width), BF16),
        V((quarter, width), F32), V((n // NC * chunks, 128), F32), V((CAP * n, width), BF16),
        V((NC * CAP, n // NC, quarter), F32), V((NC * CAP, n // NC, quarter), F32), V((quarter, width), BF16),
        V((rows_all, width), BF16), V((rows_all, cols), BF16), V((rows_all, 4 * cols), BF16),
        V((5, NX, NZ, NC, rows_out, cols), BF16), V((5, NX, NZ, rows_out, cols), BF16),
        V((NX - 1, 5, NZ, rows_out, cols), BF16), V((NX - 1, 5, NZ, rows_out, cols), BF16),
        V((5, NZ, rows_out, cols), BF16), V((NZ - 1, 5, rows_out, cols), BF16),
        V((CAP * n, rows_cat), BF16), V((CAP * n, 128), BF16),
        dma((2,)), dma((2,)), dma((NC, 2)), dma((NC, 2)), dma((2,)),
        dma((2, NM - 1)), dma((2, NM - 1)), dma((2, 4)),
        dma((2, NX)), dma((2, NX - 1)), dma((2, NZ - 1)),
    ]
    return pl.pallas_call(
        step_kernel,
        out_shape=(sds((rows_cat, width), F32), sds((4, rows_out, cols), F32), sds((rows_out, cols), F32)),
        in_specs=[SM, SM, VM, VM, VM] + [anyw] * 4,
        out_specs=(anyw, VM, VM),
        scratch_shapes=scratch,
        compiler_params=params(collective_id=0, has_side_effects=True),
        name="step",
    )(source, lengths, source_2d, owners_t, rows_t, history, catalogue, w_in, w_out)


def per_device(history, lengths, source, owners, item_rows, catalogue, w_in, w_out):
    cat_grad, w_in_grad, w_out_grad = step(
        source,
        lengths,
        source.reshape(-1, 128),
        owners.T,
        item_rows.T,
        history,
        catalogue,
        w_in,
        w_out,
    )
    return (w_in_grad, w_out_grad.T, cat_grad)


def solution(mesh):
    split = Mesh(mesh.devices.reshape(NX, NZ, NC, NM), ALL)
    placed = (
        P(DP, None, "mp"),
        P(),
        P(),
        P(ALL, None),
        P(ALL, None),
        P(ALL, None),
        P(None, None, "mp"),
        P("mp", None),
    )
    return jax.shard_map(
        per_device,
        mesh=split,
        in_specs=placed,
        out_specs=(P(None, DP, "mp"), P("mp", DP), P(ALL, None)),
        check_vma=False,
    )
```
